32 devices in a mesh: gx: 4 (over y, x), gy: 8 (over z, core).
Axes of the slice: x: 2, y: 2, z: 4, core: 2. Of those that a mesh axis runs over, the one named last changes fastest.
Arguments:
- coords: float32 [3, 4, 8, 512], P(None, 'gx', 'gy'), may hold values from 0 to 16, as said below
- neighbours: int32 [4, 8, 4, 256], P('gx', 'gy'), may hold values from -1 to 4607, as said below
- noise_var: float32 [4, 8, 512], P('gx', 'gy'), may hold values from 0.05 to 0.5
- observations: float32 [4, 8, 512], P('gx', 'gy'), may hold values from -15 to 15
Outputs:
- posterior_mean: float32 [4, 8, 512], P('gx', 'gy')
- residual: float32 [4, 8, 512], P('gx', 'gy')
The draws below stay inside these ranges and needn't reach their ends.
Inputs may be any that keep to these rules, and one draw needn't show every extreme that they name: `coords`: for point p of tile (a, b) in block j = p // 128, coordinate 0 lies in [a * 2 + j // 2, a * 2 + j // 2 + 1), coordinate 1 in [b * 2 + j % 2, b * 2 + j % 2 + 1), and coordinate 2 in [0, 4). `neighbours`: each block's list names distinct points inside the grid, in the blocks of the up to eight cells that share a side or a corner with its own cell, all of which come before it in one fixed strict order of all blocks; entries -1 are empty and come after the others.
All inputs are finite; a program needn't handle non-finite values.
Results may differ from the reference program's by a relative error of at most 0.0003.
Values sent between devices are 32-bit elements; how exact they have to be, the bound alone decides.
A program may use at most 64 MiB of HBM per device.

```python
import math
import jax
import jax.numpy as jnp
from jax import lax

CELLS = 2
BLOCK = 128
NEIGH = 256
ITERS = 2
TX = 4
TY = 8
P_TILE = 512


def draw_coords(key, part):
    unit = jax.random.uniform(key, (3, TX, TY, P_TILE), jnp.float32)
    cell_of = jnp.arange(P_TILE, dtype=jnp.int32) // BLOCK
    first = (jnp.arange(TX, dtype=jnp.int32)[:, None, None] * CELLS + (cell_of // CELLS)[None, None, :]).astype(jnp.float32) + unit[0]
    second = (jnp.arange(TY, dtype=jnp.int32)[None, :, None] * CELLS + (cell_of % CELLS)[None, None, :]).astype(jnp.float32) + unit[1]
    third = 4.0 * unit[2]
    return jnp.stack([first, second, third])


def draw_neighbours(key, part):
    side_x = TX * CELLS
    side_y = TY * CELLS
    count = 8 * BLOCK
    order_key, score_key = jax.random.split(key)
    ranks = jax.random.permutation(order_key, side_x * side_y).astype(jnp.int32).reshape(side_x, side_y)
    cell_x = jnp.arange(side_x, dtype=jnp.int32)[:, None]
    cell_y = jnp.arange(side_y, dtype=jnp.int32)[None, :]
    eligible_list = []
    base_list = []
    for step_x in (-1, 0, 1):
        for step_y in (-1, 0, 1):
            if step_x == 0 and step_y == 0:
                continue
            near_x = cell_x + step_x
            near_y = cell_y + step_y
            valid = (near_x >= 0) & (near_x < side_x) & (near_y >= 0) & (near_y < side_y)
            clip_x = jnp.clip(near_x, 0, side_x - 1)
            clip_y = jnp.clip(near_y, 0, side_y - 1)
            earlier = valid & (ranks[clip_x, clip_y] < ranks)
            offset_x = clip_x // CELLS - cell_x // CELLS + 1
            offset_y = clip_y // CELLS - cell_y // CELLS + 1
            base = (offset_x * 3 + offset_y) * P_TILE + (clip_x % CELLS * CELLS + clip_y % CELLS) * BLOCK
            eligible_list.append(earlier)
            base_list.append(jnp.broadcast_to(base, (side_x, side_y)))
    eligible = jnp.stack(eligible_list, axis=2)
    bases = jnp.stack(base_list, axis=2)
    candidates = (bases[:, :, :, None] + jnp.arange(BLOCK, dtype=jnp.int32)[None, None, None, :]).reshape(side_x, side_y, count)
    allowed = jnp.broadcast_to(eligible[:, :, :, None], (side_x, side_y, 8, BLOCK)).reshape(side_x, side_y, count)
    scores = jax.random.randint(score_key, (side_x, side_y, count), 0, 65536, dtype=jnp.int32)
    keyed = (scores + allowed.astype(jnp.int32) * 131072) * count + jnp.arange(count, dtype=jnp.int32)
    top_values, top_positions = lax.top_k(keyed, NEIGH)
    chosen = jnp.take_along_axis(candidates, top_positions, axis=2)
    chosen_live = jnp.take_along_axis(allowed, top_positions, axis=2)
    result = jnp.where(chosen_live, chosen, -1).astype(jnp.int32)
    return result.reshape(TX, CELLS, TY, CELLS, NEIGH).transpose(0, 2, 1, 3, 4).reshape(TX, TY, CELLS * CELLS, NEIGH)


def draw_observations(key, part):
    across = jnp.arange(TX, dtype=jnp.float32)[:, None, None] / max(TX - 1, 1) + jnp.arange(TY, dtype=jnp.float32)[None, :, None] / max(TY - 1, 1)
    scale = 1.0 + across
    values = jnp.clip(jax.random.normal(key, (TX, TY, P_TILE), jnp.float32), -5.0, 5.0)
    return values * scale


def steps_of(rng, shape, pieces, low, largest):
    loudness = 1.0
    for axis_at, parts in pieces:
        steps = jax.random.uniform(jax.random.fold_in(jax.random.fold_in(rng, 6), axis_at), (parts,), jnp.float32, low / len(pieces), largest / len(pieces))
        loudness = loudness * jnp.repeat(jnp.exp(steps), shape[axis_at] // parts).reshape((-1,) + (1,) * (len(shape) - 1 - axis_at))
    return loudness


def setup_inputs(seed: int = 0) -> dict:
    key_list = jax.random.split(jax.random.key(seed), 5)
    coords = draw_coords(jax.random.fold_in(key_list[4], 71), 0)
    neighbours = draw_neighbours(jax.random.fold_in(key_list[4], 71), 0)
    noise_var = jnp.clip(jnp.exp(math.log(0.5) - 2.3025851 * jax.random.uniform(key_list[2], (TX, TY, P_TILE), jnp.float32) ** steps_of(key_list[2], (TX, TY, P_TILE), ((0, 4), (1, 8)), -0.2, 0.2)), 0.05, 0.5)
    observations = draw_observations(jax.random.fold_in(key_list[4], 71), 0)
    return dict(coords=coords, neighbours=neighbours, noise_var=noise_var, observations=observations)


def kernel_value(first_x, first_y, first_t, second_x, second_y, second_t):
    distance = jnp.sqrt((first_x - second_x) ** 2 + (first_y - second_y) ** 2)
    inside = jnp.maximum(1.0 - distance, 0.0)
    return inside ** 4 * (4.0 * distance + 1.0) * jnp.exp(-jnp.abs(first_t - second_t))

def block_factors(points, noise_at, live_float, block_size):
    order = points.shape[2]
    kern = kernel_value(points[:, 0, :, None], points[:, 1, :, None], points[:, 2, :, None], points[:, 0, None, :], points[:, 1, None, :], points[:, 2, None, :])
    identity = jnp.eye(order, dtype=points.dtype)
    diagonal = live_float * noise_at + (1.0 - live_float)
    covariance = kern * live_float[:, :, None] * live_float[:, None, :] + identity[None] * diagonal[:, None, :]
    lower = jnp.linalg.cholesky(covariance)
    tail = jnp.broadcast_to(identity[:, order - block_size:], (points.shape[0], order, block_size))
    solved = lax.linalg.triangular_solve(lower, tail, left_side=True, lower=True, transpose_a=True)
    return jnp.swapaxes(solved, 1, 2)

def cell_row(coord_slab, value_slab, width):
    near_coords = jnp.stack([coord_slab[:, :, shift:shift + width] for shift in range(3)], axis=2)
    near_coords = near_coords.transpose(0, 3, 1, 2, 4).reshape(3, width, -1)
    near_values = jnp.stack([value_slab[:, shift:shift + width] for shift in range(3)], axis=1)
    near_values = near_values.transpose(2, 0, 1, 3).reshape(width, -1)
    own = coord_slab[:, 1, 1:1 + width]
    kern = kernel_value(own[0][:, :, None], own[1][:, :, None], own[2][:, :, None], near_coords[0][:, None, :], near_coords[1][:, None, :], near_coords[2][:, None, :])
    return lax.optimization_barrier(jnp.sum(kern * near_values[:, None, :], axis=2))

def reference(coords, neighbours, noise_var, observations):
    tile_points = observations.shape[2]
    tile_count = TX * TY
    blocks_tile = CELLS * CELLS
    highest = lax.Precision.HIGHEST
    flat_coords = coords.reshape(3, tile_count * tile_points)
    flat_noise = noise_var.reshape(-1)
    listed = neighbours.reshape(tile_count, blocks_tile, NEIGH).astype(jnp.int32)
    listed_live = listed >= 0
    listed_safe = jnp.maximum(listed, 0).astype(jnp.int32)
    slot = listed_safe // tile_points
    within = listed_safe % tile_points
    tile_ids = jnp.arange(tile_count, dtype=jnp.int32)[:, None, None]
    tile_a = tile_ids // TY
    tile_b = tile_ids % TY
    global_ids = ((tile_a + slot // 3 - 1) * TY + tile_b + slot % 3 - 1) * tile_points + within
    global_ids = jnp.where(listed_live, global_ids, -1).astype(jnp.int32)
    own_points = jnp.arange(tile_count, dtype=jnp.int32)[:, None, None] * tile_points + jnp.arange(tile_points, dtype=jnp.int32).reshape(1, blocks_tile, BLOCK)
    index_sets = jnp.concatenate([global_ids, own_points], axis=2)
    live_sets = index_sets >= 0
    safe_sets = jnp.maximum(index_sets, 0).astype(jnp.int32)

    def precondition(vector):

        def per_tile(entry):
            safe, live = entry
            live_float = live.astype(vector.dtype)
            points = jnp.moveaxis(flat_coords[:, safe], 0, 1)
            factors = block_factors(points, flat_noise[safe], live_float, BLOCK)
            values = vector[safe] * live_float
            whitened = jnp.einsum('bij,bj->bi', factors, values, precision=highest)
            return jnp.einsum('bij,bi->bj', factors, whitened, precision=highest) * live_float
        terms = lax.map(per_tile, (safe_sets, live_sets))
        return jnp.zeros_like(vector).at[safe_sets.reshape(-1)].add(terms.reshape(-1))
    grid_coords = coords.reshape(3, TX, TY, CELLS, CELLS, BLOCK).transpose(0, 1, 3, 2, 4, 5)
    grid_coords = grid_coords.reshape(3, TX * CELLS, TY * CELLS, BLOCK)
    padded_coords = jnp.pad(grid_coords, ((0, 0), (1, 1), (1, 1), (0, 0)))
    width = TY * CELLS

    def operate(vector):
        grid_values = vector.reshape(TX, TY, CELLS, CELLS, BLOCK).transpose(0, 2, 1, 3, 4)
        grid_values = grid_values.reshape(TX * CELLS, TY * CELLS, BLOCK)
        padded_values = jnp.pad(grid_values, ((1, 1), (1, 1), (0, 0)))

        def line(position):
            coord_slab = lax.dynamic_slice_in_dim(padded_coords, position, 3, 1)
            value_slab = lax.dynamic_slice_in_dim(padded_values, position, 3, 0)
            return cell_row(coord_slab, value_slab, width)
        lines = lax.map(line, jnp.arange(TX * CELLS, dtype=jnp.int32))
        back = lines.reshape(TX, CELLS, TY, CELLS, BLOCK).transpose(0, 2, 1, 3, 4).reshape(-1)
        return back + flat_noise * vector
    flat_obs = observations.reshape(-1)
    solution = jnp.zeros_like(flat_obs)
    residual = flat_obs
    search = precondition(residual)
    direction = search
    current = jnp.sum(residual * search)
    for step in range(ITERS):
        image = operate(direction)
        alpha = current / jnp.sum(direction * image)
        solution = solution + alpha * direction
        residual = residual - alpha * image
        if step + 1 < ITERS:
            search = precondition(residual)
            following = jnp.sum(residual * search)
            direction = search + following / current * direction
            current = following
    posterior_mean = flat_obs - flat_noise * solution
    return (posterior_mean.reshape(observations.shape), residual.reshape(observations.shape))
```

```python
import functools

import jax
import jax.numpy as jnp
from jax import lax
from jax.experimental import pallas as pl
from jax.experimental.pallas import tpu as pltpu
from jax.sharding import PartitionSpec as P

MESH = pl.DeviceIdType.MESH
BLOCK = 128
NEIGH = 256
HIGH = lax.Precision.HIGHEST
DIRS = [(dx, dy) for dx in (-1, 0, 1) for dy in (-1, 0, 1) if (dx, dy) != (0, 0)]
OWN = [5, 6, 9, 10]


def around(b):
    r, c = 1 + b // 2, 1 + b % 2
    return [(r - 1 + q // 3) * 4 + c - 1 + q % 3 for q in range(9)]


def others(b):
    return [cell for q, cell in enumerate(around(b)) if q != 4]


class Links:
    def __init__(self, nx, ny):
        self.nx, self.ny = nx, ny
        self.x, self.y = lax.axis_index("gx"), lax.axis_index("gy")

    def there(self, k):
        dx, dy = DIRS[k]
        px, py = self.x + dx, self.y + dy
        return (px >= 0) & (px < self.nx) & (py >= 0) & (py < self.ny)

    def ident(self, k):
        return (self.x + DIRS[k][0], self.y + DIRS[k][1])

    def copy(self, k, slot, src, dst, send, recv):
        return pltpu.make_async_remote_copy(
            src_ref=src,
            dst_ref=dst.at[slot],
            send_sem=send.at[k],
            recv_sem=recv.at[slot],
            device_id=self.ident(k),
            device_id_type=MESH,
        )

    def start(self, src, dst, send, recv):
        for k in range(8):

            @pl.when(self.there(k))
            def _():
                self.copy(k, 7 - k, src, dst, send, recv).start()

            @pl.when(jnp.logical_not(self.there(k)))
            def _():
                dst[k] = jnp.zeros(dst.shape[1:], dst.dtype)

    def finish(self, src, dst, send, recv):
        for k in range(8):

            @pl.when(self.there(k))
            def _():
                desc = self.copy(k, k, src, dst, send, recv)
                desc.wait_send()
                desc.wait_recv()

    def greet(self, barrier, ways=range(8)):
        count = 0
        for k in ways:
            count = count + self.there(k).astype(jnp.int32)

            @pl.when(self.there(k))
            def _():
                pl.semaphore_signal(
                    barrier, inc=1, device_id=self.ident(k), device_id_type=MESH
                )

        return count


def source_of(cell):
    row, col = cell // 4 + 1, cell % 4 + 1
    dx, dy = row // 2 - 1, col // 2 - 1
    return (dx, dy), (row % 2) * 2 + col % 2


def halo_kernel(nx, ny, coords, noise, obs, out, own, land, send, recv):
    links = Links(nx, ny)
    barrier = pltpu.get_barrier_semaphore()
    greeted = links.greet(barrier)
    own[...] = jnp.zeros_like(own)
    for axis in range(3):
        own[axis : axis + 1, :] = coords[axis, 0]
    own[3:4, :] = noise[...]
    own[4:5, :] = obs[...]
    pl.semaphore_wait(barrier, greeted)
    links.start(own, land, send, recv)
    links.finish(own, land, send, recv)
    for cell in range(16):
        way, inner = source_of(cell)
        part = slice(inner * BLOCK, (inner + 1) * BLOCK)
        value = own[:, part] if way == (0, 0) else land[DIRS.index(way), :, part]
        out[:, cell * BLOCK : (cell + 1) * BLOCK] = value


def kernel_value(ax, ay, at, bx, by, bt):
    dx, dy = ax - bx, ay - by
    distance = jnp.sqrt(dx * dx + dy * dy)
    inside = jnp.maximum(1.0 - distance, 0.0)
    square = inside * inside
    return square * square * (4.0 * distance + 1.0) * jnp.exp(-jnp.abs(at - bt))


def thirds(x):
    high = x.astype(jnp.bfloat16).astype(jnp.float32)
    rest = x - high
    mid = rest.astype(jnp.bfloat16).astype(jnp.float32)
    return high, mid, rest - mid


def dot(a, b, rhs=0):
    return lax.dot_general(
        a, b, (((1,), (rhs,)), ((), ())), precision=HIGH, preferred_element_type=jnp.float32
    )


def pick(a, b, rhs=0):
    return lax.dot_general(
        a, b, (((1,), (rhs,)), ((), ())), preferred_element_type=jnp.float32
    )


def iota(shape, axis):
    return lax.broadcasted_iota(jnp.int32, shape, axis)


def outer(n, u):
    return lax.dot_general(
        n, u, (((0,), (0,)), ((), ())), precision=HIGH, preferred_element_type=jnp.float32
    )


def whiten(a_ref, count, room):
    f32 = jnp.float32
    lanes = iota((1, BLOCK), 1)

    def spread(x, j):
        return jnp.broadcast_to(x[:, j : j + 1], (8, BLOCK))

    def tile(place, i):
        at = (place * 32 + i) * 8
        return slice(at, at + 8)

    def unpack(place, b):
        return [room[pl.ds((place * 4 + g) * 64 + b, 8, stride=8), :] for g in range(4)]

    for base in range(0, BLOCK, 32):
        for g in range(4):
            for b in range(8):
                at = base + 8 * g
                room[pl.ds(g * 64 + b, 8, stride=8), :] = a_ref[b % count, at : at + 8, :]
        rows = [room[tile(0, i), :] for i in range(32)]
        for p in range(4):
            at = base + 8 * p
            panel = rows[8 * p : 8 * p + 8]
            inside = (lanes >= at) & (lanes < at + 8)
            d = [[spread(panel[i], at + j) for j in range(i + 1)] for i in range(8)]
            y = [jnp.where(inside, (lanes == at + i).astype(f32), panel[i]) for i in range(8)]
            low = [[None] * 8 for _ in range(8)]
            inverse = [None] * 8
            for j in range(8):
                inverse[j] = 1.0 / d[j][j]
                for i in range(j + 1, 8):
                    low[i][j] = d[i][j] * inverse[j]
                for i in range(j + 1, 8):
                    for k in range(j + 1, i + 1):
                        d[i][k] = d[i][k] - low[i][j] * d[k][j]
                for i in range(j + 1, 8):
                    y[i] = y[i] - low[i][j] * y[j]
            for i in range(8):
                scaled = y[i] * lax.rsqrt(d[i][i])
                room[tile(3, p * 8 + i), :] = jnp.where(lanes < at + 8, scaled, 0.0)
            if at == BLOCK - 8:
                break
            u = [y[j] * inverse[j] for j in range(8)]
            for j in range(7, 0, -1):
                for i in range(j):
                    u[i] = u[i] - low[j][i] * u[j]
            later = (lanes >= at + 8) & (lanes < base + 32)
            for i in range(8):
                room[tile(1, p * 8 + i), :] = panel[i]
                room[tile(2, p * 8 + i), :] = jnp.where(later, 0.0, u[i])
            for r in range(8 * p + 8, 32):
                t = [spread(rows[r], at + k) * u[k] for k in range(8)]
                total = ((t[0] + t[1]) + (t[2] + t[3])) + ((t[4] + t[5]) + (t[6] + t[7]))
                rows[r] = jnp.where(inside, 0.0, rows[r]) - total
        within = (lanes >= base) & (lanes < base + 32)
        for b in range(count):
            if base + 32 < BLOCK:
                n, u = (jnp.concatenate(unpack(place, b), axis=0) for place in (1, 2))
                below = jnp.where(within, 0.0, a_ref[b, base + 32 :, :])
                a_ref[b, base + 32 :, :] = below - outer(n, u)[base + 32 :, :]
            a_ref[b, base : base + 32, :] = jnp.concatenate(unpack(3, b), axis=0)


def factor_kernel(f_ref, listed_ref, m_ref, a_ref, hot, c11, c21, c22, x1, l21, room):
    count = 4
    listed = listed_ref[0, 0]
    slot, within = listed >> 9, listed & 511
    third = (slot * 11) >> 5
    row = third * 2 + (within >> 8) - 1
    col = (slot - 3 * third) * 2 + ((within >> 7) & 1) - 1
    index = jnp.where(listed >= 0, (row * 4 + col) * BLOCK + (within & 127), -1)
    idx = index.astype(jnp.float32)
    idx = jnp.concatenate([idx, idx], axis=0)
    idx_t = idx.T
    lane = iota((1, BLOCK), 1).astype(jnp.float32)
    for b in range(count):
        chosen = idx_t[:, b : b + 1]
        for q, cell in enumerate(others(b)):
            same = chosen == lane + float(cell * BLOCK)
            hot[b, :, q * BLOCK : (q + 1) * BLOCK] = same.astype(jnp.float32).astype(jnp.bfloat16)
        near = jnp.concatenate(
            [f_ref[:, cell * BLOCK : (cell + 1) * BLOCK] for cell in others(b)], axis=1
        )
        stacked = jnp.concatenate([*thirds(near), jnp.zeros_like(near)], axis=0)
        found = pick(stacked.astype(jnp.bfloat16), hot[b], 1)
        x = found[0:8] + found[8:16] + found[16:24]
        xt = x.T
        live_row = (idx[b : b + 1, :] >= 0.0).astype(jnp.float32)
        live_col = (chosen >= 0.0).astype(jnp.float32)
        diagonal = live_row * x[3:4] + (1.0 - live_row)
        on_diagonal = iota((NEIGH, NEIGH), 0) == iota((NEIGH, NEIGH), 1)
        kern = kernel_value(xt[:, 0:1], xt[:, 1:2], xt[:, 2:3], x[0:1], x[1:2], x[2:3])
        c11[b] = kern * live_col * live_row + jnp.where(on_diagonal, diagonal, 0.0)
        home = OWN[b] * BLOCK
        o = f_ref[:, home : home + BLOCK]
        ot = o.T
        kern = kernel_value(ot[:, 0:1], ot[:, 1:2], ot[:, 2:3], x[0:1], x[1:2], x[2:3])
        c21[b] = kern * live_row
        on_diagonal = iota((BLOCK, BLOCK), 0) == iota((BLOCK, BLOCK), 1)
        kern = kernel_value(ot[:, 0:1], ot[:, 1:2], ot[:, 2:3], o[0:1], o[1:2], o[2:3])
        c22[b] = kern + jnp.where(on_diagonal, o[3:4], 0.0)
        a_ref[b] = c11[b, 0:BLOCK, 0:BLOCK]
    whiten(a_ref, count, room)
    for b in range(count):
        first = a_ref[b]
        x1[b] = first
        below = jnp.concatenate([c11[b, BLOCK:, 0:BLOCK], c21[b, :, 0:BLOCK]], axis=0)
        left = dot(below, first, 1)
        upper = left[0:BLOCK]
        l21[b] = upper
        change = dot(left, upper, 1)
        a_ref[b] = c11[b, BLOCK:, BLOCK:] - change[0:BLOCK]
        c21[b, :, BLOCK:] = c21[b, :, BLOCK:] - change[BLOCK:]
        c21[b, :, 0:BLOCK] = left[BLOCK:]
        c22[b] = c22[b] - dot(left[BLOCK:], left[BLOCK:], 1)
    whiten(a_ref, count, room)
    for b in range(count):
        second = a_ref[b]
        l32 = dot(c21[b, :, BLOCK:], second, 1)
        a_ref[b] = c22[b] - dot(l32, l32, 1)
        b2 = dot(l32, second)
        c21[b, :, BLOCK:] = b2
        c21[b, :, 0:BLOCK] = dot(c21[b, :, 0:BLOCK] - dot(b2, l21[b]), x1[b])
    whiten(a_ref, count, room)
    for b in range(count):
        third = a_ref[b]
        compact = -dot(third, c21[b])
        stacked = jnp.concatenate(thirds(compact), axis=0).astype(jnp.bfloat16)
        wide = pick(stacked, hot[b])
        wide = wide[0:BLOCK] + wide[BLOCK : 2 * BLOCK] + wide[2 * BLOCK :]
        m_ref[b, :, 0 : 4 * BLOCK] = wide[:, : 4 * BLOCK]
        m_ref[b, :, 4 * BLOCK : 5 * BLOCK] = third
        m_ref[b, :, 5 * BLOCK :] = wide[:, 4 * BLOCK :]


def solve_kernel(nx, ny, f_ref, m_ref, mean_ref, res_ref, k_ref, *scratch):
    (res, terms, terms_in, total, image, image_in, sums, sums_y, sums_x) = scratch[:9]
    (send_t, recv_t, send_i, recv_i, send_y, recv_y, send_x, recv_x) = scratch[9:]
    links = Links(nx, ny)
    gx, gy = links.x, links.y
    direct = nx * ny <= 64
    barrier = pltpu.get_barrier_semaphore()
    if direct:
        me, size = gx * ny + gy, nx * ny
        places = [lax.rem(me + off, size) for off in range(1, size)]
        line_y = [(lax.div(at, ny), lax.rem(at, ny)) for at in places]
        line_x, greeted = [], size - 1
    else:
        me, size = gy, ny
        greeted = links.greet(barrier, [k for k in range(8) if 0 not in DIRS[k]]) + nx + ny - 2
        line_y = [(gx, lax.rem(gy + off, ny)) for off in range(1, ny)]
        line_x = [(lax.rem(gx + off, nx), gy) for off in range(1, nx)]
    for peer in line_y + line_x:
        pl.semaphore_signal(barrier, inc=1, device_id=peer, device_id_type=MESH)
    for cell in range(16):
        res[cell : cell + 1, :] = f_ref[4:5, cell * BLOCK : (cell + 1) * BLOCK]
    noise = [f_ref[3:4, c * BLOCK : (c + 1) * BLOCK] for c in OWN]

    def precondition(step):
        out = [jnp.zeros((1, BLOCK), jnp.float32) for _ in range(16)]
        for b in range(4):
            acc = jnp.zeros((BLOCK, BLOCK), jnp.float32)
            for q, cell in enumerate(around(b)):
                acc = acc + m_ref[b, :, q * BLOCK : (q + 1) * BLOCK] * res[cell : cell + 1, :]
            w = jnp.sum(acc, axis=1, keepdims=True)
            for q, cell in enumerate(around(b)):
                part = m_ref[b, :, q * BLOCK : (q + 1) * BLOCK] * w
                out[cell] = out[cell] + jnp.sum(part, axis=0, keepdims=True)
        for cell in range(16):
            terms[step, cell : cell + 1, :] = out[cell]

    def fill_kernel():
        parts = [f_ref[:, cell * BLOCK : (cell + 1) * BLOCK] for cell in range(16)]
        turned = [part.T for part in parts]
        for b in range(4):
            o = parts[OWN[b]]
            for q, cell in enumerate(around(b)):
                t = turned[cell]
                kern = kernel_value(t[:, 0:1], t[:, 1:2], t[:, 2:3], o[0:1], o[1:2], o[2:3])
                k_ref[b, q * BLOCK : (q + 1) * BLOCK, :] = kern

    def exchange_terms(step):
        args = (terms.at[step], terms_in.at[step], send_t.at[step], recv_t.at[step])
        links.start(*args)
        if step == 0:
            fill_kernel()
        links.finish(*args)
        for cell in range(16):
            r, c = cell // 4, cell % 4
            value = terms[step, cell : cell + 1, :]
            for k, (dx, dy) in enumerate(DIRS):
                rr, cc = r - 2 * dx, c - 2 * dy
                if 0 <= rr < 4 and 0 <= cc < 4:
                    at = rr * 4 + cc
                    value = value + terms_in[step, k, at : at + 1, :]
            if step == 1:
                value = value - total[0, cell : cell + 1, :]
            total[step, cell : cell + 1, :] = value

    def operate(step):
        columns = total[step].T
        for b in range(4):
            acc = jnp.zeros((BLOCK, BLOCK), jnp.float32)
            for q, cell in enumerate(around(b)):
                acc = acc + k_ref[b, q * BLOCK : (q + 1) * BLOCK, :] * columns[:, cell : cell + 1]
            value = jnp.sum(acc, axis=0, keepdims=True)
            value = value + noise[b] * total[step, OWN[b] : OWN[b] + 1, :]
            image[step, b : b + 1, :] = value

    def line_copy(src, buf, send, recv, peer, at, off):
        return pltpu.make_async_remote_copy(
            src_ref=src,
            dst_ref=buf.at[at],
            send_sem=send.at[off],
            recv_sem=recv.at[off],
            device_id=peer,
            device_id_type=MESH,
        )

    def reduce_line(src, buf, send, recv, peers, me, size):
        copies = [line_copy(src, buf, send, recv, p, me, o) for o, p in enumerate(peers)]
        for copy in copies:
            copy.start()
        buf[me] = src[...]
        for copy in copies:
            copy.wait()
        value = buf[0]
        for at in range(1, size):
            value = value + buf[at]
        return value

    def reduce_all(rows):
        lanes = iota((1, BLOCK), 1)
        packed = jnp.zeros((1, BLOCK), jnp.float32)
        for at, row in enumerate(rows):
            packed = packed + jnp.where(lanes == at, jnp.sum(row, axis=1, keepdims=True), 0.0)
        sums[0] = packed
        value = reduce_line(sums.at[0], sums_y, send_y, recv_y, line_y, me, size)
        if not direct:
            sums[1] = value
            value = reduce_line(sums.at[1], sums_x, send_x, recv_x, line_x, gx, nx)
        return [
            jnp.sum(jnp.where(lanes == at, value, 0.0), axis=1, keepdims=True)
            for at in range(len(rows))
        ]

    def across(left, right):
        value = left[0] * right[0]
        for a, b in zip(left[1:], right[1:]):
            value = value + a * b
        return value

    def mine(ref, step):
        return [ref[step, c : c + 1, :] for c in OWN]

    precondition(0)
    pl.semaphore_wait(barrier, greeted)
    exchange_terms(0)
    image[...] = jnp.zeros_like(image)
    operate(0)
    args = (image.at[0], image_in, send_i, recv_i)
    links.start(*args)
    first = mine(total, 0)
    along = [image[0, b : b + 1, :] for b in range(4)]
    start = [res[c : c + 1, :] for c in OWN]
    links.finish(*args)
    for cell in range(16):
        way, inner = source_of(cell)
        if way == (0, 0):
            value = image[0, inner : inner + 1, :]
        else:
            value = image_in[DIRS.index(way), inner : inner + 1, :]
        res[cell : cell + 1, :] = value
    precondition(1)
    exchange_terms(1)
    operate(1)
    second = mine(total, 1)
    along2 = [image[1, b : b + 1, :] for b in range(4)]
    base, extra, cross, curve = reduce_all(
        [
            across(first, along),
            across([s - a for s, a in zip(start, along)], first),
            across(along, second),
            across(second, along2),
        ]
    )
    share = extra / base
    alpha = 1.0 + share
    kappa = alpha * cross / base
    alpha2 = (share + kappa) * base / (alpha * (curve - cross * cross / base))
    for b in range(4):
        solved = alpha * first[b] + alpha2 * (kappa * first[b] - alpha * second[b])
        mean_ref[b : b + 1, :] = start[b] - noise[b] * solved
        left = start[b] - alpha * along[b]
        res_ref[b : b + 1, :] = left - alpha2 * (kappa * along[b] - alpha * along2[b])


def local(nx, ny, coords, neighbours, noise_var, observations):
    tile = observations.shape[2]
    line = nx * ny if nx * ny <= 64 else ny
    f32 = jnp.float32
    vmem = pl.BlockSpec(memory_space=pltpu.VMEM)
    dma = pltpu.SemaphoreType.DMA
    patch = pl.pallas_call(
        functools.partial(halo_kernel, nx, ny),
        out_shape=jax.ShapeDtypeStruct((8, 16 * BLOCK), f32),
        in_specs=[vmem] * 3,
        out_specs=vmem,
        scratch_shapes=[
            pltpu.VMEM((8, tile), f32),
            pltpu.VMEM((8, 8, tile), f32),
            dma((8,)),
            dma((8,)),
        ],
        compiler_params=pltpu.CompilerParams(collective_id=0, has_side_effects=True),
        name="halo",
    )(coords, noise_var.reshape(1, tile), observations.reshape(1, tile))
    wide = jax.ShapeDtypeStruct((4, BLOCK, 9 * BLOCK), f32)
    square = pltpu.VMEM((4, BLOCK, BLOCK), f32)
    m = pl.pallas_call(
        factor_kernel,
        out_shape=wide,
        in_specs=[vmem] * 2,
        out_specs=vmem,
        scratch_shapes=[
            square,
            pltpu.VMEM((4, NEIGH, 8 * BLOCK), jnp.bfloat16),
            pltpu.VMEM((4, NEIGH, NEIGH), f32),
            pltpu.VMEM((4, BLOCK, NEIGH), f32),
            square,
            square,
            square,
            pltpu.VMEM((1024, BLOCK), f32),
        ],
        compiler_params=pltpu.CompilerParams(vmem_limit_bytes=48 << 20),
        name="factor",
    )(patch, neighbours)
    mean, residual = pl.pallas_call(
        functools.partial(solve_kernel, nx, ny),
        out_shape=(jax.ShapeDtypeStruct((4, BLOCK), f32),) * 2,
        in_specs=[vmem] * 2,
        out_specs=[vmem] * 2,
        scratch_shapes=[
            pltpu.VMEM((4, 9 * BLOCK, BLOCK), f32),
            pltpu.VMEM((16, BLOCK), f32),
            pltpu.VMEM((2, 16, BLOCK), f32),
            pltpu.VMEM((2, 8, 16, BLOCK), f32),
            pltpu.VMEM((2, 16, BLOCK), f32),
            pltpu.VMEM((2, 8, BLOCK), f32),
            pltpu.VMEM((8, 8, BLOCK), f32),
            pltpu.VMEM((2, 1, BLOCK), f32),
            pltpu.VMEM((line, 1, BLOCK), f32),
            pltpu.VMEM((nx, 1, BLOCK), f32),
            dma((2, 8)),
            dma((2, 8)),
            dma((8,)),
            dma((8,)),
            dma((line,)),
            dma((line,)),
            dma((nx,)),
            dma((nx,)),
        ],
        compiler_params=pltpu.CompilerParams(
            collective_id=1, has_side_effects=True, vmem_limit_bytes=48 << 20
        ),
        name="solve",
    )(patch, m)
    return (mean.reshape(observations.shape), residual.reshape(observations.shape))


def solution(mesh):
    in_specs = (
        P(None, "gx", "gy", None),
        P("gx", "gy", None, None),
        P("gx", "gy", None),
        P("gx", "gy", None),
    )
    out_specs = (P("gx", "gy", None), P("gx", "gy", None))
    body = functools.partial(local, mesh.shape["gx"], mesh.shape["gy"])
    return jax.shard_map(body, mesh=mesh, in_specs=in_specs, out_specs=out_specs, check_vma=False)
```

```python
import functools

import jax
import jax.numpy as jnp
from jax import lax
from jax.experimental import pallas as pl
from jax.experimental.pallas import tpu as pltpu
from jax.sharding import PartitionSpec as P

MESH = pl.DeviceIdType.MESH
BLOCK = 128
NEIGH = 256
HALF = 64
HIGH = lax.Precision.HIGHEST
DIRS = [(dx, dy) for dx in (-1, 0, 1) for dy in (-1, 0, 1) if (dx, dy) != (0, 0)]
OWN = [5, 6, 9, 10]


def around(b):
    r, c = 1 + b // 2, 1 + b % 2
    return [(r - 1 + q // 3) * 4 + c - 1 + q % 3 for q in range(9)]


def others(b):
    return [cell for q, cell in enumerate(around(b)) if q != 4]


class Links:
    def __init__(self, nx, ny):
        self.nx, self.ny = nx, ny
        self.x, self.y = lax.axis_index("gx"), lax.axis_index("gy")

    def there(self, k):
        dx, dy = DIRS[k]
        px, py = self.x + dx, self.y + dy
        return (px >= 0) & (px < self.nx) & (py >= 0) & (py < self.ny)

    def ident(self, k):
        return (self.x + DIRS[k][0], self.y + DIRS[k][1])

    def copy(self, k, slot, src, dst, send, recv):
        return pltpu.make_async_remote_copy(
            src_ref=src,
            dst_ref=dst.at[slot],
            send_sem=send.at[k],
            recv_sem=recv.at[slot],
            device_id=self.ident(k),
            device_id_type=MESH,
        )

    def start(self, src, dst, send, recv):
        for k in range(8):

            @pl.when(self.there(k))
            def _():
                self.copy(k, 7 - k, src, dst, send, recv).start()

            @pl.when(jnp.logical_not(self.there(k)))
            def _():
                dst[k] = jnp.zeros(dst.shape[1:], dst.dtype)

    def finish(self, src, dst, send, recv):
        for k in range(8):

            @pl.when(self.there(k))
            def _():
                desc = self.copy(k, k, src, dst, send, recv)
                desc.wait_send()
                desc.wait_recv()

    def greet(self, barrier, ways=range(8)):
        count = 0
        for k in ways:
            count = count + self.there(k).astype(jnp.int32)

            @pl.when(self.there(k))
            def _():
                pl.semaphore_signal(
                    barrier, inc=1, device_id=self.ident(k), device_id_type=MESH
                )

        return count


def source_of(cell):
    row, col = cell // 4 + 1, cell % 4 + 1
    dx, dy = row // 2 - 1, col // 2 - 1
    return (dx, dy), (row % 2) * 2 + col % 2


def kernel_value(ax, ay, at, bx, by, bt):
    dx, dy = ax - bx, ay - by
    distance = jnp.sqrt(dx * dx + dy * dy)
    inside = jnp.maximum(1.0 - distance, 0.0)
    square = inside * inside
    return square * square * (4.0 * distance + 1.0) * jnp.exp(-jnp.abs(at - bt))


def thirds(x):
    high = x.astype(jnp.bfloat16).astype(jnp.float32)
    rest = x - high
    mid = rest.astype(jnp.bfloat16).astype(jnp.float32)
    return high, mid, rest - mid


def dot(a, b, rhs=0):
    return lax.dot_general(
        a, b, (((1,), (rhs,)), ((), ())), precision=HIGH, preferred_element_type=jnp.float32
    )


def pick(a, b, rhs=0):
    return lax.dot_general(
        a, b, (((1,), (rhs,)), ((), ())), preferred_element_type=jnp.float32
    )


def iota(shape, axis):
    return lax.broadcasted_iota(jnp.int32, shape, axis)


def blockdiag(x, first):
    return jnp.concatenate([jnp.where(first, x, 0.0), jnp.where(first, 0.0, x)], axis=0)


def whiten(pair):
    f32 = jnp.float32
    lane = iota((8, BLOCK), 1)
    group, column = lane & HALF, lane & (HALF - 1)
    sub = iota((8, BLOCK), 0)

    def take(x, at):
        return jnp.take_along_axis(x, group + at, axis=1)

    def row(x, j):
        return jnp.broadcast_to(x[j : j + 1, :], (8, BLOCK))

    pair = [list(rows) for rows in pair]
    out = [[None] * 8 for _ in pair]
    for p in range(8):
        at = 8 * p
        inside = (column >= at) & (column < at + 8)
        for h, rows in enumerate(pair):
            g = [take(rows[p], at + j) for j in range(8)]
            y = jnp.where(inside, (column == at + sub).astype(f32), rows[p])
            later = [[take(rows[v], at + j) for j in range(8)] for v in range(p + 1, 8)]
            rest = [jnp.where(inside, 0.0, rows[v]) for v in range(p + 1, 8)]
            pivots, inverses = row(g[0], 0), None
            for j in range(8):
                pivot = row(g[j], j)
                inverse = 1.0 / pivot
                pivots = pivot if j == 0 else jnp.where(sub == j, pivot, pivots)
                inverses = inverse if j == 0 else jnp.where(sub == j, inverse, inverses)
                low = jnp.where(sub > j, g[j] * inverse, 0.0)
                across = [row(g[k], j) for k in range(j + 1, 8)]
                here = row(y, j)
                if j < 7:
                    y = y - low * here
                for k in range(j + 1, 8):
                    g[k] = g[k] - low * across[k - j - 1]
                if p < 7:
                    e = later[0]
                    low = e[j] * inverse
                    rest[0] = rest[0] - low * here
                    for k in range(j + 1, 8):
                        e[k] = e[k] - low * across[k - j - 1]
            out[h][p] = jnp.where(column < at + 8, y * lax.rsqrt(pivots), 0.0)
            if p < 6:
                u = y * inverses
                for j in range(7, 0, -1):
                    u = u - jnp.where(sub < j, g[j] * inverses, 0.0) * row(u, j)
                spread = [row(u, k) for k in range(8)]
                for v in range(1, 7 - p):
                    t = [later[v][k] * spread[k] for k in range(8)]
                    total = ((t[0] + t[1]) + (t[2] + t[3])) + ((t[4] + t[5]) + (t[6] + t[7]))
                    rest[v] = rest[v] - total
            for v in range(p + 1, 8):
                rows[v] = rest[v - p - 1]
    return [jnp.concatenate(rows, axis=0) for rows in out]


def halves(even, odd, c, first):
    tile = slice(c // 2 * BLOCK, (c // 2 + 1) * BLOCK)
    even, odd = even[:, tile], odd[:, tile]
    if c % 2 == 0:
        odd = pltpu.roll(odd, HALF, axis=1)
    else:
        even = pltpu.roll(even, HALF, axis=1)
    return jnp.where(first, even, odd)


def factor(cc, ll, xx, gg, g_ref, first):
    def own_part():
        for h in range(2):
            after = []
            for c in range(3, -1, -1):
                value = ll[h, c, 4 * HALF :]
                if after:
                    left = jnp.concatenate([gg[h, k] for k in after], axis=1)
                    right = jnp.concatenate(
                        [blockdiag(ll[h, c, k * HALF : (k + 1) * HALF], first) for k in after],
                        axis=0,
                    )
                    value = value - dot(left, right)
                gg[h, c] = dot(value, blockdiag(xx[h, c], first))
                after.append(c)

    for c in range(6):
        at, then = c * HALF, (c + 1) * HALF
        tiles = [[cc[h, c, at + 8 * v : at + 8 * v + 8] for v in range(8)] for h in range(2)]
        found = whiten(tiles)
        for h in range(2):
            xx[h, c] = found[h]
        if c == 5:
            break
        spread = [blockdiag(x, first) for x in found]
        for h in range(2):
            left = dot(cc[h, c, then : then + HALF], spread[h], 1)
            ll[h, c, then : then + HALF] = left
            change = dot(left, blockdiag(left, first), 1)
            cc[h, c + 1, then : then + HALF] = cc[h, c + 1, then : then + HALF] - change
        if c < 4:
            after = then + HALF
            for h in range(2):
                ll[h, c, after:] = dot(cc[h, c, after:], spread[h], 1)
            for other in range(c + 1, 6):
                start = other * HALF
                top = after if other == c + 1 else start
                for h in range(2):
                    right = blockdiag(ll[h, c, start : start + HALF], first)
                    change = dot(ll[h, c, top:], right, 1)
                    cc[h, other, top:] = cc[h, other, top:] - change
        if c == 3:
            own_part()
    for h in range(2):
        x4, x5 = xx[h, 4], xx[h, 5]
        l54 = ll[h, 4, 5 * HALF :]
        right = jnp.concatenate([blockdiag(gg[h, c, 0:HALF], first) for c in range(4)], axis=1)
        upper = -dot(x4, right)
        upper = [upper[:, c * BLOCK : (c + 1) * BLOCK] for c in range(4)] + [x4]
        right = jnp.concatenate([blockdiag(x, first) for x in upper], axis=1)
        mixed = dot(l54, right)
        mixed = [mixed[:, c * BLOCK : (c + 1) * BLOCK] for c in range(5)]
        mixed = [mixed[c] + gg[h, c, HALF:] for c in range(4)] + [mixed[4]]
        right = jnp.concatenate([blockdiag(x, first) for x in mixed], axis=1)
        lower = -dot(x5, right)
        lower = [lower[:, c * BLOCK : (c + 1) * BLOCK] for c in range(5)] + [x5]
        upper = upper + [jnp.zeros_like(x5)]
        for c in range(6):
            g_ref[h, c, 0:HALF] = upper[c]
            g_ref[h, c, HALF:] = lower[c]


def solve_kernel(nx, ny, *refs):
    (coords, listed_hbm, noise_hbm, obs_hbm, mean_ref, res_ref) = refs[:6]
    (own, land, listed_ref, f_ref, hot, cc, ll, xx, gg, g_ref, seen, k_ref) = refs[6:18]
    (res, terms, terms_in, total, image, image_in, sums, sums_y, sums_x) = refs[18:27]
    (load, send_h, recv_h, send_t, recv_t, send_i, recv_i) = refs[27:34]
    (send_y, recv_y, send_x, recv_x) = refs[34:]
    f32 = jnp.float32
    links = Links(nx, ny)
    gx, gy = links.x, links.y
    direct = nx * ny <= 64
    barrier = pltpu.get_barrier_semaphore()
    if direct:
        me, size = gx * ny + gy, nx * ny
        places = [lax.rem(me + off, size) for off in range(1, size)]
        line_y = [(lax.div(at, ny), lax.rem(at, ny)) for at in places]
        line_x, greeted = [], size - 1
    else:
        me, size = gy, ny
        greeted = links.greet(barrier, [k for k in range(8) if 0 not in DIRS[k]]) + nx + ny - 2
        line_y = [(gx, lax.rem(gy + off, ny)) for off in range(1, ny)]
        line_x = [(lax.rem(gx + off, nx), gy) for off in range(1, nx)]
    for peer in line_y + line_x:
        pl.semaphore_signal(barrier, inc=1, device_id=peer, device_id_type=MESH)
    loads = [
        pltpu.make_async_copy(coords.at[axis, 0], own.at[axis : axis + 1], load.at[axis])
        for axis in range(3)
    ]
    loads.append(pltpu.make_async_copy(noise_hbm, own.at[3:4], load.at[3]))
    loads.append(pltpu.make_async_copy(obs_hbm, own.at[4:5], load.at[4]))
    loads.append(pltpu.make_async_copy(listed_hbm.at[0, 0], listed_ref, load.at[5]))
    for copy in loads:
        copy.start()
    own[5:8] = jnp.zeros((3, own.shape[1]), f32)
    image[...] = jnp.zeros_like(image)
    for copy in loads:
        copy.wait()
    pl.semaphore_wait(barrier, greeted)
    halo = (own, land, send_h, recv_h)
    links.start(*halo)

    lane = iota((1, BLOCK), 1)
    front = lane < HALF
    listed = listed_ref[...]
    slot, within = listed >> 9, listed & 511
    third = (slot * 11) >> 5
    row = third * 2 + (within >> 8) - 1
    col = (slot - 3 * third) * 2 + ((within >> 7) & 1) - 1
    index = jnp.where(listed >= 0, (row * 4 + col) * BLOCK + (within & 127), -1)
    idx = index.astype(f32)
    idx_t = jnp.concatenate([idx, idx], axis=0).T
    lane_f = lane.astype(f32)
    away = []
    for h in range(2):
        for s in range(2):
            chosen = idx_t[:, 2 * h + s : 2 * h + s + 1]
            for q, cell in enumerate(others(2 * h + s)):
                same = (chosen == lane_f + float(cell * BLOCK)).astype(f32).astype(jnp.bfloat16)
                for c in range(4):
                    at = c * BLOCK + s * HALF
                    part = same[c * HALF : (c + 1) * HALF]
                    hot[h, at : at + HALF, q * BLOCK : (q + 1) * BLOCK] = part
        even, odd = idx[2 * h : 2 * h + 1], idx[2 * h + 1 : 2 * h + 2]
        dead = jnp.concatenate([halves(even, odd, c, front) for c in range(4)], axis=1) < 0.0
        away.append(jnp.where(dead, 1000.0 * (iota((1, 4 * BLOCK), 1) + 1).astype(f32), 0.0))

    links.finish(*halo)
    for cell in range(16):
        way, inner = source_of(cell)
        part = slice(inner * BLOCK, (inner + 1) * BLOCK)
        value = own[:, part] if way == (0, 0) else land[DIRS.index(way), :, part]
        f_ref[:, cell * BLOCK : (cell + 1) * BLOCK] = value
    for cell in range(16):
        res[cell : cell + 1, :] = f_ref[4:5, cell * BLOCK : (cell + 1) * BLOCK]
    noise = [f_ref[3:4, c * BLOCK : (c + 1) * BLOCK] for c in OWN]

    def gather(h, even, odd):
        n = even.shape[0]
        rows = [*thirds(even), *thirds(odd)]
        fill = (-6 * n) % 16
        if fill:
            rows.append(jnp.zeros((fill, even.shape[1]), f32))
        found = pick(jnp.concatenate(rows, axis=0).astype(jnp.bfloat16), hot[h], 1)
        even = found[0:n] + found[n : 2 * n] + found[2 * n : 3 * n]
        odd = found[3 * n : 4 * n] + found[4 * n : 5 * n] + found[5 * n : 6 * n]
        return jnp.where((iota((1, 4 * BLOCK), 1) & HALF) == 0, even, odd)

    for h in range(2):
        near = [
            jnp.concatenate(
                [f_ref[:, cell * BLOCK : (cell + 1) * BLOCK] for cell in others(2 * h + s)], axis=1
            )
            for s in range(2)
        ]
        x = gather(h, *near)
        seen[h, 0:4] = jnp.concatenate(
            [x[4:5, c * BLOCK : (c + 1) * BLOCK] for c in range(4)], axis=0
        )
        x = jnp.where(iota((8, 4 * BLOCK), 0) == 0, x + away[h], x)
        mine = [f_ref[:, OWN[2 * h + s] * BLOCK : (OWN[2 * h + s] + 1) * BLOCK] for s in range(2)]
        x = jnp.concatenate([x] + [halves(*mine, c, front) for c in range(2)], axis=1)
        seen[h, 4:6] = jnp.concatenate(
            [x[4:5, c * BLOCK : (c + 1) * BLOCK] for c in range(4, 6)], axis=0
        )
        t = x.T
        even_t, odd_t = (
            jnp.concatenate(
                [t[c * BLOCK + s * HALF : c * BLOCK + (s + 1) * HALF] for c in range(6)], axis=0
            )
            for s in range(2)
        )
        down = [jnp.where(front, even_t[:, a : a + 1], odd_t[:, a : a + 1]) for a in range(3)]
        for c in range(6):
            o = x[:, c * BLOCK : (c + 1) * BLOCK]
            at = c * HALF
            kern = kernel_value(*[d[at:] for d in down], o[0:1], o[1:2], o[2:3])
            diagonal = iota((HALF, BLOCK), 0) == (iota((HALF, BLOCK), 1) & (HALF - 1))
            cc[h, c, at : at + HALF] = kern[:HALF] + jnp.where(diagonal, o[3:4], 0.0)
            if c < 5:
                cc[h, c, at + HALF :] = kern[HALF:]
    factor(cc, ll, xx, gg, g_ref, front)

    def precondition(step):
        out = [jnp.zeros((1, BLOCK), f32) for _ in range(16)]
        for h in range(2):
            ends = (2 * h, 2 * h + 1)
            if step == 0:
                v = [seen[h, c : c + 1, :] for c in range(6)]
            else:
                near = [jnp.concatenate([res[c : c + 1] for c in others(b)], axis=1) for b in ends]
                found = gather(h, *near)
                v = [found[:, c * BLOCK : (c + 1) * BLOCK] for c in range(4)]
                mine = [res[OWN[b] : OWN[b] + 1] for b in ends]
                v = v + [halves(*mine, c, front) for c in range(2)]
            acc = g_ref[h, 0] * v[0]
            for c in range(1, 6):
                acc = acc + g_ref[h, c] * v[c]
            even = jnp.sum(jnp.where(front, acc, 0.0), axis=1, keepdims=True)
            odd = jnp.sum(jnp.where(front, 0.0, acc), axis=1, keepdims=True)
            w = jnp.where(front, even, odd)
            t = [jnp.sum(g_ref[h, c] * w, axis=0, keepdims=True) for c in range(6)]
            wide = jnp.concatenate(t[0:4], axis=1)
            half = (iota((1, 4 * BLOCK), 1) & HALF) == 0
            rows = [*thirds(jnp.where(half, wide, 0.0)), *thirds(jnp.where(half, 0.0, wide))]
            rows.append(jnp.zeros((10, 4 * BLOCK), f32))
            found = pick(jnp.concatenate(rows, axis=0).astype(jnp.bfloat16), hot[h])
            turned = [pltpu.roll(x, HALF, axis=1) for x in t[4:6]]
            kept = [jnp.where(front, t[4], turned[1]), jnp.where(front, turned[0], t[5])]
            for s, b in enumerate(ends):
                value = found[3 * s : 3 * s + 1] + found[3 * s + 1 : 3 * s + 2]
                value = value + found[3 * s + 2 : 3 * s + 3]
                for q, cell in enumerate(others(b)):
                    out[cell] = out[cell] + value[:, q * BLOCK : (q + 1) * BLOCK]
                out[OWN[b]] = out[OWN[b]] + kept[s]
        for cell in range(16):
            terms[step, cell : cell + 1, :] = out[cell]

    def fill_kernel():
        parts = [f_ref[:, cell * BLOCK : (cell + 1) * BLOCK] for cell in range(16)]
        turned = [part.T for part in parts]
        for b in range(4):
            o = parts[OWN[b]]
            for q, cell in enumerate(around(b)):
                t = turned[cell]
                kern = kernel_value(t[:, 0:1], t[:, 1:2], t[:, 2:3], o[0:1], o[1:2], o[2:3])
                k_ref[b, q * BLOCK : (q + 1) * BLOCK, :] = kern

    def exchange_terms(step):
        args = (terms.at[step], terms_in.at[step], send_t.at[step], recv_t.at[step])
        links.start(*args)
        if step == 0:
            fill_kernel()
        links.finish(*args)
        for cell in range(16):
            r, c = cell // 4, cell % 4
            value = terms[step, cell : cell + 1, :]
            for k, (dx, dy) in enumerate(DIRS):
                rr, cc = r - 2 * dx, c - 2 * dy
                if 0 <= rr < 4 and 0 <= cc < 4:
                    at = rr * 4 + cc
                    value = value + terms_in[step, k, at : at + 1, :]
            if step == 1:
                value = value - total[0, cell : cell + 1, :]
            total[step, cell : cell + 1, :] = value

    def operate(step):
        columns = total[step].T
        for b in range(4):
            acc = jnp.zeros((BLOCK, BLOCK), jnp.float32)
            for q, cell in enumerate(around(b)):
                acc = acc + k_ref[b, q * BLOCK : (q + 1) * BLOCK, :] * columns[:, cell : cell + 1]
            value = jnp.sum(acc, axis=0, keepdims=True)
            value = value + noise[b] * total[step, OWN[b] : OWN[b] + 1, :]
            image[step, b : b + 1, :] = value

    def line_copy(src, buf, send, recv, peer, at, off):
        return pltpu.make_async_remote_copy(
            src_ref=src,
            dst_ref=buf.at[at],
            send_sem=send.at[off],
            recv_sem=recv.at[off],
            device_id=peer,
            device_id_type=MESH,
        )

    def reduce_line(src, buf, send, recv, peers, me, size):
        copies = [line_copy(src, buf, send, recv, p, me, o) for o, p in enumerate(peers)]
        for copy in copies:
            copy.start()
        buf[me] = src[...]
        for copy in copies:
            copy.wait()
        value = buf[0]
        for at in range(1, size):
            value = value + buf[at]
        return value

    def reduce_all(rows):
        lanes = iota((1, BLOCK), 1)
        packed = jnp.zeros((1, BLOCK), jnp.float32)
        for at, row in enumerate(rows):
            packed = packed + jnp.where(lanes == at, jnp.sum(row, axis=1, keepdims=True), 0.0)
        sums[0] = packed
        value = reduce_line(sums.at[0], sums_y, send_y, recv_y, line_y, me, size)
        if not direct:
            sums[1] = value
            value = reduce_line(sums.at[1], sums_x, send_x, recv_x, line_x, gx, nx)
        return [
            jnp.sum(jnp.where(lanes == at, value, 0.0), axis=1, keepdims=True)
            for at in range(len(rows))
        ]

    def across(left, right):
        value = left[0] * right[0]
        for a, b in zip(left[1:], right[1:]):
            value = value + a * b
        return value

    def mine(ref, step):
        return [ref[step, c : c + 1, :] for c in OWN]

    precondition(0)
    exchange_terms(0)
    operate(0)
    args = (image.at[0], image_in, send_i, recv_i)
    links.start(*args)
    first = mine(total, 0)
    along = [image[0, b : b + 1, :] for b in range(4)]
    start = [res[c : c + 1, :] for c in OWN]
    links.finish(*args)
    for cell in range(16):
        way, inner = source_of(cell)
        if way == (0, 0):
            value = image[0, inner : inner + 1, :]
        else:
            value = image_in[DIRS.index(way), inner : inner + 1, :]
        res[cell : cell + 1, :] = value
    precondition(1)
    exchange_terms(1)
    operate(1)
    second = mine(total, 1)
    along2 = [image[1, b : b + 1, :] for b in range(4)]
    base, extra, cross, curve = reduce_all(
        [
            across(first, along),
            across([s - a for s, a in zip(start, along)], first),
            across(along, second),
            across(second, along2),
        ]
    )
    share = extra / base
    alpha = 1.0 + share
    kappa = alpha * cross / base
    alpha2 = (share + kappa) * base / (alpha * (curve - cross * cross / base))
    for b in range(4):
        solved = alpha * first[b] + alpha2 * (kappa * first[b] - alpha * second[b])
        mean_ref[b : b + 1, :] = start[b] - noise[b] * solved
        left = start[b] - alpha * along[b]
        res_ref[b : b + 1, :] = left - alpha2 * (kappa * along[b] - alpha * along2[b])


def local(nx, ny, coords, neighbours, noise_var, observations):
    tile = observations.shape[2]
    line = nx * ny if nx * ny <= 64 else ny
    f32 = jnp.float32
    vmem = pl.BlockSpec(memory_space=pltpu.VMEM)
    dma = pltpu.SemaphoreType.DMA
    whole = pl.BlockSpec(memory_space=pl.ANY)
    mean, residual = pl.pallas_call(
        functools.partial(solve_kernel, nx, ny),
        out_shape=(jax.ShapeDtypeStruct((4, BLOCK), f32),) * 2,
        in_specs=[whole] * 4,
        out_specs=[vmem] * 2,
        scratch_shapes=[
            pltpu.VMEM((8, tile), f32),
            pltpu.VMEM((8, 8, tile), f32),
            pltpu.VMEM((4, NEIGH), jnp.int32),
            pltpu.VMEM((8, 16 * BLOCK), f32),
            pltpu.VMEM((2, 4 * BLOCK, 8 * BLOCK), jnp.bfloat16),
            pltpu.VMEM((2, 6, 6 * HALF, BLOCK), f32),
            pltpu.VMEM((2, 5, 6 * HALF, BLOCK), f32),
            pltpu.VMEM((2, 6, HALF, BLOCK), f32),
            pltpu.VMEM((2, 4, BLOCK, BLOCK), f32),
            pltpu.VMEM((2, 6, BLOCK, BLOCK), f32),
            pltpu.VMEM((2, 8, BLOCK), f32),
            pltpu.VMEM((4, 9 * BLOCK, BLOCK), f32),
            pltpu.VMEM((16, BLOCK), f32),
            pltpu.VMEM((2, 16, BLOCK), f32),
            pltpu.VMEM((2, 8, 16, BLOCK), f32),
            pltpu.VMEM((2, 16, BLOCK), f32),
            pltpu.VMEM((2, 8, BLOCK), f32),
            pltpu.VMEM((8, 8, BLOCK), f32),
            pltpu.VMEM((2, 1, BLOCK), f32),
            pltpu.VMEM((line, 1, BLOCK), f32),
            pltpu.VMEM((nx, 1, BLOCK), f32),
            dma((6,)),
            dma((8,)),
            dma((8,)),
            dma((2, 8)),
            dma((2, 8)),
            dma((8,)),
            dma((8,)),
            dma((line,)),
            dma((line,)),
            dma((nx,)),
            dma((nx,)),
        ],
        compiler_params=pltpu.CompilerParams(
            collective_id=0, has_side_effects=True, vmem_limit_bytes=60 << 20
        ),
        name="solve",
    )(coords, neighbours, noise_var.reshape(1, tile), observations.reshape(1, tile))
    return (mean.reshape(observations.shape), residual.reshape(observations.shape))


def solution(mesh):
    in_specs = (
        P(None, "gx", "gy", None),
        P("gx", "gy", None, None),
        P("gx", "gy", None),
        P("gx", "gy", None),
    )
    out_specs = (P("gx", "gy", None), P("gx", "gy", None))
    body = functools.partial(local, mesh.shape["gx"], mesh.shape["gy"])
    return jax.shard_map(body, mesh=mesh, in_specs=in_specs, out_specs=out_specs, check_vma=False)
```

```python
import functools

import jax
import jax.numpy as jnp
from jax import lax
from jax.experimental import pallas as pl
from jax.experimental.pallas import tpu as pltpu
from jax.sharding import PartitionSpec as P

MESH = pl.DeviceIdType.MESH
BLOCK = 128
NEIGH = 256
HALF = 64
HIGH = lax.Precision.HIGHEST
DIRS = [(dx, dy) for dx in (-1, 0, 1) for dy in (-1, 0, 1) if (dx, dy) != (0, 0)]
OWN = [5, 6, 9, 10]
FAR_FIRST = [0, 2, 5, 7, 1, 6, 3, 4]


def around(b):
    r, c = 1 + b // 2, 1 + b % 2
    return [(r - 1 + q // 3) * 4 + c - 1 + q % 3 for q in range(9)]


def others(b):
    return [cell for q, cell in enumerate(around(b)) if q != 4]


class Links:
    def __init__(self, nx, ny):
        self.nx, self.ny = nx, ny
        self.x, self.y = lax.axis_index("gx"), lax.axis_index("gy")

    def there(self, k):
        dx, dy = DIRS[k]
        px, py = self.x + dx, self.y + dy
        return (px >= 0) & (px < self.nx) & (py >= 0) & (py < self.ny)

    def ident(self, k):
        return (self.x + DIRS[k][0], self.y + DIRS[k][1])

    def copy(self, k, slot, src, dst, send, recv, part):
        return pltpu.make_async_remote_copy(
            src_ref=src.at[part],
            dst_ref=dst.at[(slot, *part)],
            send_sem=send.at[k],
            recv_sem=recv.at[slot],
            device_id=self.ident(k),
            device_id_type=MESH,
        )

    def start(self, src, dst, send, recv, cut):
        for k in FAR_FIRST:

            @pl.when(self.there(k))
            def _():
                self.copy(k, 7 - k, src, dst, send, recv, cut(k)).start()

        for k in range(8):

            @pl.when(jnp.logical_not(self.there(k)))
            def _():
                dst[k] = jnp.zeros(dst.shape[1:], dst.dtype)

    def finish(self, src, dst, send, recv, cut):
        for k in range(8):

            @pl.when(self.there(k))
            def _():
                self.copy(k, k, src, dst, send, recv, cut(k)).wait_send()
                self.copy(k, k, src, dst, send, recv, cut(7 - k)).wait_recv()

    def far(self, k, reach):
        px, py = self.x + DIRS[k][0] * reach, self.y + DIRS[k][1] * reach
        return (px >= 0) & (px < self.nx) & (py >= 0) & (py < self.ny), (px, py)

    def tell(self, sem, reach):
        for k in range(8):
            exists, peer = self.far(k, reach)

            @pl.when(exists)
            def _():
                pl.semaphore_signal(sem, inc=1, device_id=peer, device_id_type=MESH)

    def hear(self, sem, reach):
        count = 0
        for k in range(8):
            count = count + self.far(k, reach)[0].astype(jnp.int32)
        pl.semaphore_wait(sem, count)

    def greet(self, barrier, ways=range(8)):
        count = 0
        for k in ways:
            count = count + self.there(k).astype(jnp.int32)

            @pl.when(self.there(k))
            def _():
                pl.semaphore_signal(
                    barrier, inc=1, device_id=self.ident(k), device_id_type=MESH
                )

        return count


def halo_cut(k):
    dx, dy = DIRS[k]
    if dx == 0:
        return (slice(0, 8), slice(0, 4 * BLOCK))
    at, wide = (0, 2) if dy == 0 else (max(dy, 0), 1)
    at = (at + 2 * max(dx, 0)) * BLOCK
    return (slice(0, 8), slice(at, at + wide * BLOCK))


def terms_cut(k):
    rows = {-1: slice(0, 8), 0: slice(0, 16), 1: slice(8, 16)}[DIRS[k][0]]
    return (rows, slice(0, BLOCK))


def image_cut(k):
    return (slice(0, 8), slice(0, BLOCK))


def source_of(cell):
    row, col = cell // 4 + 1, cell % 4 + 1
    dx, dy = row // 2 - 1, col // 2 - 1
    return (dx, dy), (row % 2) * 2 + col % 2


def kernel_value(ax, ay, at, bx, by, bt):
    dx, dy = ax - bx, ay - by
    distance = jnp.sqrt(dx * dx + dy * dy)
    inside = jnp.maximum(1.0 - distance, 0.0)
    square = inside * inside
    return square * square * (4.0 * distance + 1.0) * jnp.exp(-jnp.abs(at - bt))


def thirds(x):
    high = x.astype(jnp.bfloat16).astype(jnp.float32)
    rest = x - high
    mid = rest.astype(jnp.bfloat16).astype(jnp.float32)
    return high, mid, rest - mid


def dot(a, b, rhs=0):
    (a1, a2, a3), (b1, b2, b3) = (
        [x.astype(jnp.bfloat16) for x in thirds(y)] for y in (a, b)
    )
    left = jnp.concatenate([a1, a1, a2, a1, a3, a2], axis=1)
    right = jnp.concatenate([b1, b2, b1, b3, b1, b2], axis=rhs)
    return pick(left, right, rhs)


def pick(a, b, rhs=0):
    return lax.dot_general(
        a, b, (((1,), (rhs,)), ((), ())), preferred_element_type=jnp.float32
    )


def iota(shape, axis):
    return lax.broadcasted_iota(jnp.int32, shape, axis)


def blockdiag(x, first):
    return jnp.concatenate([jnp.where(first, x, 0.0), jnp.where(first, 0.0, x)], axis=0)


def whiten(pair):
    f32 = jnp.float32
    lane = iota((8, BLOCK), 1)
    group, column = lane & HALF, lane & (HALF - 1)
    sub = iota((8, BLOCK), 0)

    def take(x, at):
        return jnp.take_along_axis(x, group + at, axis=1)

    def row(x, j):
        return jnp.broadcast_to(x[j : j + 1, :], (8, BLOCK))

    pair = [list(rows) for rows in pair]
    out = [[None] * 8 for _ in pair]
    for p in range(8):
        at = 8 * p
        inside = (column >= at) & (column < at + 8)
        for h, rows in enumerate(pair):
            g = [take(rows[p], at + j) for j in range(8)]
            y = jnp.where(inside, (column == at + sub).astype(f32), rows[p])
            later = [[take(rows[v], at + j) for j in range(8)] for v in range(p + 1, 8)]
            rest = [jnp.where(inside, 0.0, rows[v]) for v in range(p + 1, 8)]
            pivots, inverses = row(g[0], 0), None
            for j in range(8):
                pivot = row(g[j], j)
                inverse = 1.0 / pivot
                pivots = pivot if j == 0 else jnp.where(sub == j, pivot, pivots)
                inverses = inverse if j == 0 else jnp.where(sub == j, inverse, inverses)
                low = jnp.where(sub > j, g[j] * inverse, 0.0)
                across = [row(g[k], j) for k in range(j + 1, 8)]
                here = row(y, j)
                if j < 7:
                    y = y - low * here
                for k in range(j + 1, 8):
                    g[k] = g[k] - low * across[k - j - 1]
                if p < 7:
                    e = later[0]
                    low = e[j] * inverse
                    rest[0] = rest[0] - low * here
                    for k in range(j + 1, 8):
                        e[k] = e[k] - low * across[k - j - 1]
            out[h][p] = jnp.where(column < at + 8, y * lax.rsqrt(pivots), 0.0)
            if p < 6:
                u = y * inverses
                for j in range(7, 0, -1):
                    u = u - jnp.where(sub < j, g[j] * inverses, 0.0) * row(u, j)
                spread = [row(u, k) for k in range(8)]
                for v in range(1, 7 - p):
                    t = [later[v][k] * spread[k] for k in range(8)]
                    total = ((t[0] + t[1]) + (t[2] + t[3])) + ((t[4] + t[5]) + (t[6] + t[7]))
                    rest[v] = rest[v] - total
            for v in range(p + 1, 8):
                rows[v] = rest[v - p - 1]
    return [jnp.concatenate(rows, axis=0) for rows in out]


def halves(even, odd, c, first):
    tile = slice(c // 2 * BLOCK, (c // 2 + 1) * BLOCK)
    even, odd = even[:, tile], odd[:, tile]
    if c % 2 == 0:
        odd = pltpu.roll(odd, HALF, axis=1)
    else:
        even = pltpu.roll(even, HALF, axis=1)
    return jnp.where(first, even, odd)


def factor(cc, ll, xx, gg, g_ref, first):
    def own_part():
        for h in range(2):
            after = []
            for c in range(3, -1, -1):
                value = ll[h, c, 4 * HALF :]
                if after:
                    left = jnp.concatenate([gg[h, k] for k in after], axis=1)
                    right = jnp.concatenate(
                        [blockdiag(ll[h, c, k * HALF : (k + 1) * HALF], first) for k in after],
                        axis=0,
                    )
                    value = value - dot(left, right)
                gg[h, c] = dot(value, blockdiag(xx[h, c], first))
                after.append(c)

    for c in range(6):
        at, then = c * HALF, (c + 1) * HALF
        tiles = [[cc[h, c, at + 8 * v : at + 8 * v + 8] for v in range(8)] for h in range(2)]
        found = whiten(tiles)
        for h in range(2):
            xx[h, c] = found[h]
        if c == 5:
            break
        spread = [blockdiag(x, first) for x in found]
        for h in range(2):
            left = dot(cc[h, c, then : then + HALF], spread[h], 1)
            ll[h, c, then : then + HALF] = left
            change = dot(left, blockdiag(left, first), 1)
            cc[h, c + 1, then : then + HALF] = cc[h, c + 1, then : then + HALF] - change
        if c < 4:
            after = then + HALF
            for h in range(2):
                ll[h, c, after:] = dot(cc[h, c, after:], spread[h], 1)
            for other in range(c + 1, 6):
                start = other * HALF
                top = after if other == c + 1 else start
                for h in range(2):
                    right = blockdiag(ll[h, c, start : start + HALF], first)
                    change = dot(ll[h, c, top:], right, 1)
                    cc[h, other, top:] = cc[h, other, top:] - change
        if c == 3:
            own_part()
    for h in range(2):
        x4, x5 = xx[h, 4], xx[h, 5]
        l54 = ll[h, 4, 5 * HALF :]
        right = jnp.concatenate([blockdiag(gg[h, c, 0:HALF], first) for c in range(4)], axis=1)
        upper = -dot(x4, right)
        upper = [upper[:, c * BLOCK : (c + 1) * BLOCK] for c in range(4)] + [x4]
        right = jnp.concatenate([blockdiag(x, first) for x in upper], axis=1)
        mixed = dot(l54, right)
        mixed = [mixed[:, c * BLOCK : (c + 1) * BLOCK] for c in range(5)]
        mixed = [mixed[c] + gg[h, c, HALF:] for c in range(4)] + [mixed[4]]
        right = jnp.concatenate([blockdiag(x, first) for x in mixed], axis=1)
        lower = -dot(x5, right)
        lower = [lower[:, c * BLOCK : (c + 1) * BLOCK] for c in range(5)] + [x5]
        upper = upper + [jnp.zeros_like(x5)]
        for c in range(6):
            g_ref[h, c, 0:HALF] = upper[c]
            g_ref[h, c, HALF:] = lower[c]


def solve_kernel(nx, ny, *refs):
    (coords, listed_hbm, noise_hbm, obs_hbm, mean_ref, res_ref) = refs[:6]
    (own, land, listed_ref, f_ref, hot, cc, ll, xx, gg, g_ref, seen, k_ref) = refs[6:18]
    (res, terms, terms_in, total, image, image_in, sums, sums_y, sums_x) = refs[18:27]
    (load, send_h, recv_h, send_t, recv_t, send_i, recv_i) = refs[27:34]
    (send_y, recv_y, send_x, recv_x, known) = refs[34:]
    f32 = jnp.float32
    links = Links(nx, ny)
    gx, gy = links.x, links.y
    direct = max(nx, ny) <= 8
    barrier = pltpu.get_barrier_semaphore()
    if direct:
        me, size = gx * ny + gy, nx * ny
        places = [lax.rem(me + off, size) for off in range(1, size)]
        line_y = [(lax.div(at, ny), lax.rem(at, ny)) for at in places]
        line_x, greeted = [], links.greet(barrier)
    else:
        me, size = gy, ny
        greeted = links.greet(barrier, [k for k in range(8) if 0 not in DIRS[k]]) + nx + ny - 2
        line_y = [(gx, lax.rem(gy + off, ny)) for off in range(1, ny)]
        line_x = [(lax.rem(gx + off, nx), gy) for off in range(1, nx)]
    for peer in [] if direct else line_y + line_x:
        pl.semaphore_signal(barrier, inc=1, device_id=peer, device_id_type=MESH)
    loads = [
        pltpu.make_async_copy(coords.at[axis, 0], own.at[axis : axis + 1], load.at[axis])
        for axis in range(3)
    ]
    loads.append(pltpu.make_async_copy(noise_hbm, own.at[3:4], load.at[3]))
    loads.append(pltpu.make_async_copy(obs_hbm, own.at[4:5], load.at[4]))
    loads.append(pltpu.make_async_copy(listed_hbm.at[0, 0], listed_ref, load.at[5]))
    for copy in loads:
        copy.start()
    own[5:8] = jnp.zeros((3, own.shape[1]), f32)
    image[...] = jnp.zeros_like(image)
    for copy in loads:
        copy.wait()
    pl.semaphore_wait(barrier, greeted)
    reaches = [1 << r for r in range(3)] if direct else []
    if direct:
        links.tell(known.at[0], 1)

    def widen(r):
        if direct:
            links.hear(known.at[r], reaches[r])
            if r < 2:
                links.tell(known.at[r + 1], reaches[r + 1])

    halo = (own, land, send_h, recv_h, halo_cut)
    links.start(*halo)

    lane = iota((1, BLOCK), 1)
    front = lane < HALF
    listed = listed_ref[...]
    slot, within = listed >> 9, listed & 511
    third = (slot * 11) >> 5
    row = third * 2 + (within >> 8) - 1
    col = (slot - 3 * third) * 2 + ((within >> 7) & 1) - 1
    index = jnp.where(listed >= 0, (row * 4 + col) * BLOCK + (within & 127), -1)
    idx = index.astype(f32)
    idx_t = jnp.concatenate([idx, idx], axis=0).T
    lane_f = lane.astype(f32)
    away = []
    for h in range(2):
        for s in range(2):
            chosen = idx_t[:, 2 * h + s : 2 * h + s + 1]
            for q, cell in enumerate(others(2 * h + s)):
                same = (chosen == lane_f + float(cell * BLOCK)).astype(f32).astype(jnp.bfloat16)
                for c in range(4):
                    at = c * BLOCK + s * HALF
                    part = same[c * HALF : (c + 1) * HALF]
                    hot[h, at : at + HALF, q * BLOCK : (q + 1) * BLOCK] = part
        even, odd = idx[2 * h : 2 * h + 1], idx[2 * h + 1 : 2 * h + 2]
        dead = jnp.concatenate([halves(even, odd, c, front) for c in range(4)], axis=1) < 0.0
        away.append(jnp.where(dead, 1000.0 * (iota((1, 4 * BLOCK), 1) + 1).astype(f32), 0.0))

    links.finish(*halo)
    for cell in range(16):
        way, inner = source_of(cell)
        part = slice(inner * BLOCK, (inner + 1) * BLOCK)
        value = own[:, part] if way == (0, 0) else land[DIRS.index(way), :, part]
        f_ref[:, cell * BLOCK : (cell + 1) * BLOCK] = value
    for cell in range(16):
        res[cell : cell + 1, :] = f_ref[4:5, cell * BLOCK : (cell + 1) * BLOCK]
    noise = [f_ref[3:4, c * BLOCK : (c + 1) * BLOCK] for c in OWN]

    def gather(h, even, odd):
        n = even.shape[0]
        rows = [*thirds(even), *thirds(odd)]
        fill = (-6 * n) % 16
        if fill:
            rows.append(jnp.zeros((fill, even.shape[1]), f32))
        found = pick(jnp.concatenate(rows, axis=0).astype(jnp.bfloat16), hot[h], 1)
        even = found[0:n] + found[n : 2 * n] + found[2 * n : 3 * n]
        odd = found[3 * n : 4 * n] + found[4 * n : 5 * n] + found[5 * n : 6 * n]
        return jnp.where((iota((1, 4 * BLOCK), 1) & HALF) == 0, even, odd)

    for h in range(2):
        near = [
            jnp.concatenate(
                [f_ref[:, cell * BLOCK : (cell + 1) * BLOCK] for cell in others(2 * h + s)], axis=1
            )
            for s in range(2)
        ]
        x = gather(h, *near)
        seen[h, 0:4] = jnp.concatenate(
            [x[4:5, c * BLOCK : (c + 1) * BLOCK] for c in range(4)], axis=0
        )
        x = jnp.where(iota((8, 4 * BLOCK), 0) == 0, x + away[h], x)
        mine = [f_ref[:, OWN[2 * h + s] * BLOCK : (OWN[2 * h + s] + 1) * BLOCK] for s in range(2)]
        x = jnp.concatenate([x] + [halves(*mine, c, front) for c in range(2)], axis=1)
        seen[h, 4:6] = jnp.concatenate(
            [x[4:5, c * BLOCK : (c + 1) * BLOCK] for c in range(4, 6)], axis=0
        )
        t = x.T
        even_t, odd_t = (
            jnp.concatenate(
                [t[c * BLOCK + s * HALF : c * BLOCK + (s + 1) * HALF] for c in range(6)], axis=0
            )
            for s in range(2)
        )
        down = [jnp.where(front, even_t[:, a : a + 1], odd_t[:, a : a + 1]) for a in range(3)]
        for c in range(6):
            o = x[:, c * BLOCK : (c + 1) * BLOCK]
            at = c * HALF
            kern = kernel_value(*[d[at:] for d in down], o[0:1], o[1:2], o[2:3])
            diagonal = iota((HALF, BLOCK), 0) == (iota((HALF, BLOCK), 1) & (HALF - 1))
            cc[h, c, at : at + HALF] = kern[:HALF] + jnp.where(diagonal, o[3:4], 0.0)
            if c < 5:
                cc[h, c, at + HALF :] = kern[HALF:]
    widen(0)
    factor(cc, ll, xx, gg, g_ref, front)
    widen(1)

    def precondition(step):
        out = [jnp.zeros((1, BLOCK), f32) for _ in range(16)]
        for h in range(2):
            ends = (2 * h, 2 * h + 1)
            if step == 0:
                v = [seen[h, c : c + 1, :] for c in range(6)]
            else:
                near = [jnp.concatenate([res[c : c + 1] for c in others(b)], axis=1) for b in ends]
                found = gather(h, *near)
                v = [found[:, c * BLOCK : (c + 1) * BLOCK] for c in range(4)]
                mine = [res[OWN[b] : OWN[b] + 1] for b in ends]
                v = v + [halves(*mine, c, front) for c in range(2)]
            acc = g_ref[h, 0] * v[0]
            for c in range(1, 6):
                acc = acc + g_ref[h, c] * v[c]
            even = jnp.sum(jnp.where(front, acc, 0.0), axis=1, keepdims=True)
            odd = jnp.sum(jnp.where(front, 0.0, acc), axis=1, keepdims=True)
            w = jnp.where(front, even, odd)
            t = [jnp.sum(g_ref[h, c] * w, axis=0, keepdims=True) for c in range(6)]
            wide = jnp.concatenate(t[0:4], axis=1)
            half = (iota((1, 4 * BLOCK), 1) & HALF) == 0
            rows = [*thirds(jnp.where(half, wide, 0.0)), *thirds(jnp.where(half, 0.0, wide))]
            rows.append(jnp.zeros((10, 4 * BLOCK), f32))
            found = pick(jnp.concatenate(rows, axis=0).astype(jnp.bfloat16), hot[h])
            turned = [pltpu.roll(x, HALF, axis=1) for x in t[4:6]]
            kept = [jnp.where(front, t[4], turned[1]), jnp.where(front, turned[0], t[5])]
            for s, b in enumerate(ends):
                value = found[3 * s : 3 * s + 1] + found[3 * s + 1 : 3 * s + 2]
                value = value + found[3 * s + 2 : 3 * s + 3]
                for q, cell in enumerate(others(b)):
                    out[cell] = out[cell] + value[:, q * BLOCK : (q + 1) * BLOCK]
                out[OWN[b]] = out[OWN[b]] + kept[s]
        for cell in range(16):
            terms[step, cell : cell + 1, :] = out[cell]

    def fill_kernel():
        parts = [f_ref[:, cell * BLOCK : (cell + 1) * BLOCK] for cell in range(16)]
        turned = [part.T for part in parts]
        for b in range(4):
            o = parts[OWN[b]]
            for q, cell in enumerate(around(b)):
                t = turned[cell]
                kern = kernel_value(t[:, 0:1], t[:, 1:2], t[:, 2:3], o[0:1], o[1:2], o[2:3])
                k_ref[b, q * BLOCK : (q + 1) * BLOCK, :] = kern

    def exchange_terms(step):
        args = (terms.at[step], terms_in.at[step], send_t.at[step], recv_t.at[step], terms_cut)
        links.start(*args)
        if step == 0:
            fill_kernel()
        links.finish(*args)
        for cell in range(16):
            r, c = cell // 4, cell % 4
            value = terms[step, cell : cell + 1, :]
            for k, (dx, dy) in enumerate(DIRS):
                rr, cc = r - 2 * dx, c - 2 * dy
                if 0 <= rr < 4 and 0 <= cc < 4:
                    at = rr * 4 + cc
                    value = value + terms_in[step, k, at : at + 1, :]
            if step == 1:
                value = value - total[0, cell : cell + 1, :]
            total[step, cell : cell + 1, :] = value

    def operate(step):
        columns = total[step].T
        for b in range(4):
            acc = jnp.zeros((BLOCK, BLOCK), jnp.float32)
            for q, cell in enumerate(around(b)):
                acc = acc + k_ref[b, q * BLOCK : (q + 1) * BLOCK, :] * columns[:, cell : cell + 1]
            value = jnp.sum(acc, axis=0, keepdims=True)
            value = value + noise[b] * total[step, OWN[b] : OWN[b] + 1, :]
            image[step, b : b + 1, :] = value

    def line_copy(src, buf, send, recv, peer, at, off):
        return pltpu.make_async_remote_copy(
            src_ref=src,
            dst_ref=buf.at[at],
            send_sem=send.at[off],
            recv_sem=recv.at[off],
            device_id=peer,
            device_id_type=MESH,
        )

    def reduce_line(src, buf, send, recv, peers, me, size):
        copies = [line_copy(src, buf, send, recv, p, me, o) for o, p in enumerate(peers)]
        for copy in copies:
            copy.start()
        buf[me] = src[...]
        for copy in copies:
            copy.wait()
        value = buf[0]
        for at in range(1, size):
            value = value + buf[at]
        return value

    def reduce_all(rows):
        lanes = iota((1, BLOCK), 1)
        packed = jnp.zeros((1, BLOCK), jnp.float32)
        for at, row in enumerate(rows):
            packed = packed + jnp.where(lanes == at, jnp.sum(row, axis=1, keepdims=True), 0.0)
        sums[0] = packed
        value = reduce_line(sums.at[0], sums_y, send_y, recv_y, line_y, me, size)
        if not direct:
            sums[1] = value
            value = reduce_line(sums.at[1], sums_x, send_x, recv_x, line_x, gx, nx)
        return [
            jnp.sum(jnp.where(lanes == at, value, 0.0), axis=1, keepdims=True)
            for at in range(len(rows))
        ]

    def across(left, right):
        value = left[0] * right[0]
        for a, b in zip(left[1:], right[1:]):
            value = value + a * b
        return value

    def mine(ref, step):
        return [ref[step, c : c + 1, :] for c in OWN]

    precondition(0)
    exchange_terms(0)
    operate(0)
    args = (image.at[0], image_in, send_i, recv_i, image_cut)
    links.start(*args)
    first = mine(total, 0)
    along = [image[0, b : b + 1, :] for b in range(4)]
    start = [res[c : c + 1, :] for c in OWN]
    links.finish(*args)
    for cell in range(16):
        way, inner = source_of(cell)
        if way == (0, 0):
            value = image[0, inner : inner + 1, :]
        else:
            value = image_in[DIRS.index(way), inner : inner + 1, :]
        res[cell : cell + 1, :] = value
    precondition(1)
    widen(2)
    exchange_terms(1)
    operate(1)
    second = mine(total, 1)
    along2 = [image[1, b : b + 1, :] for b in range(4)]
    base, extra, cross, curve = reduce_all(
        [
            across(first, along),
            across([s - a for s, a in zip(start, along)], first),
            across(along, second),
            across(second, along2),
        ]
    )
    share = extra / base
    alpha = 1.0 + share
    kappa = alpha * cross / base
    alpha2 = (share + kappa) * base / (alpha * (curve - cross * cross / base))
    for b in range(4):
        solved = alpha * first[b] + alpha2 * (kappa * first[b] - alpha * second[b])
        part = slice(b * BLOCK, (b + 1) * BLOCK)
        mean_ref[:, part] = start[b] - noise[b] * solved
        left = start[b] - alpha * along[b]
        res_ref[:, part] = left - alpha2 * (kappa * along[b] - alpha * along2[b])


def local(nx, ny, coords, neighbours, noise_var, observations):
    tile = observations.shape[2]
    line = nx * ny if max(nx, ny) <= 8 else ny
    f32 = jnp.float32
    vmem = pl.BlockSpec(memory_space=pltpu.VMEM)
    dma = pltpu.SemaphoreType.DMA
    whole = pl.BlockSpec(memory_space=pl.ANY)
    mean, residual = pl.pallas_call(
        functools.partial(solve_kernel, nx, ny),
        out_shape=(jax.ShapeDtypeStruct((1, tile), f32),) * 2,
        in_specs=[whole] * 4,
        out_specs=[vmem] * 2,
        scratch_shapes=[
            pltpu.VMEM((8, tile), f32),
            pltpu.VMEM((8, 8, tile), f32),
            pltpu.VMEM((4, NEIGH), jnp.int32),
            pltpu.VMEM((8, 16 * BLOCK), f32),
            pltpu.VMEM((2, 4 * BLOCK, 8 * BLOCK), jnp.bfloat16),
            pltpu.VMEM((2, 6, 6 * HALF, BLOCK), f32),
            pltpu.VMEM((2, 5, 6 * HALF, BLOCK), f32),
            pltpu.VMEM((2, 6, HALF, BLOCK), f32),
            pltpu.VMEM((2, 4, BLOCK, BLOCK), f32),
            pltpu.VMEM((2, 6, BLOCK, BLOCK), f32),
            pltpu.VMEM((2, 8, BLOCK), f32),
            pltpu.VMEM((4, 9 * BLOCK, BLOCK), f32),
            pltpu.VMEM((16, BLOCK), f32),
            pltpu.VMEM((2, 16, BLOCK), f32),
            pltpu.VMEM((2, 8, 16, BLOCK), f32),
            pltpu.VMEM((2, 16, BLOCK), f32),
            pltpu.VMEM((2, 8, BLOCK), f32),
            pltpu.VMEM((8, 8, BLOCK), f32),
            pltpu.VMEM((2, 1, BLOCK), f32),
            pltpu.VMEM((line, 1, BLOCK), f32),
            pltpu.VMEM((nx, 1, BLOCK), f32),
            dma((6,)),
            dma((8,)),
            dma((8,)),
            dma((2, 8)),
            dma((2, 8)),
            dma((8,)),
            dma((8,)),
            dma((line,)),
            dma((line,)),
            dma((nx,)),
            dma((nx,)),
            pltpu.SemaphoreType.REGULAR((3,)),
        ],
        compiler_params=pltpu.CompilerParams(
            collective_id=0, has_side_effects=True, vmem_limit_bytes=60 << 20
        ),
        name="solve",
    )(coords, neighbours, noise_var.reshape(1, tile), observations.reshape(1, tile))
    return (mean.reshape(observations.shape), residual.reshape(observations.shape))


def solution(mesh):
    in_specs = (
        P(None, "gx", "gy", None),
        P("gx", "gy", None, None),
        P("gx", "gy", None),
        P("gx", "gy", None),
    )
    out_specs = (P("gx", "gy", None), P("gx", "gy", None))
    body = functools.partial(local, mesh.shape["gx"], mesh.shape["gy"])
    return jax.shard_map(body, mesh=mesh, in_specs=in_specs, out_specs=out_specs, check_vma=False)
```

```python
import functools

import jax
import jax.numpy as jnp
from jax import lax
from jax.experimental import pallas as pl
from jax.experimental.pallas import tpu as pltpu
from jax.sharding import PartitionSpec as P

MESH = pl.DeviceIdType.MESH
BLOCK = 128
NEIGH = 256
HALF = 64
HIGH = lax.Precision.HIGHEST
DIRS = [(dx, dy) for dx in (-1, 0, 1) for dy in (-1, 0, 1) if (dx, dy) != (0, 0)]
OWN = [5, 6, 9, 10]
FAR_FIRST = [0, 2, 5, 7, 1, 6, 3, 4]


def around(b):
    r, c = 1 + b // 2, 1 + b % 2
    return [(r - 1 + q // 3) * 4 + c - 1 + q % 3 for q in range(9)]


def others(b):
    return [cell for q, cell in enumerate(around(b)) if q != 4]


class Links:
    def __init__(self, nx, ny):
        self.nx, self.ny = nx, ny
        self.x, self.y = lax.axis_index("gx"), lax.axis_index("gy")

    def there(self, k):
        dx, dy = DIRS[k]
        px, py = self.x + dx, self.y + dy
        return (px >= 0) & (px < self.nx) & (py >= 0) & (py < self.ny)

    def ident(self, k):
        return (self.x + DIRS[k][0], self.y + DIRS[k][1])

    def copy(self, k, slot, src, dst, send, recv, part):
        return pltpu.make_async_remote_copy(
            src_ref=src.at[part],
            dst_ref=dst.at[(slot, *part)],
            send_sem=send.at[k],
            recv_sem=recv.at[slot],
            device_id=self.ident(k),
            device_id_type=MESH,
        )

    def start(self, src, dst, send, recv, cut):
        for k in FAR_FIRST:

            @pl.when(self.there(k))
            def _():
                self.copy(k, 7 - k, src, dst, send, recv, cut(k)).start()

        for k in range(8):

            @pl.when(jnp.logical_not(self.there(k)))
            def _():
                dst[k] = jnp.zeros(dst.shape[1:], dst.dtype)

    def finish(self, src, dst, send, recv, cut):
        for k in range(8):

            @pl.when(self.there(k))
            def _():
                self.copy(k, k, src, dst, send, recv, cut(k)).wait_send()
                self.copy(k, k, src, dst, send, recv, cut(7 - k)).wait_recv()

    def far(self, k, reach):
        px, py = self.x + DIRS[k][0] * reach, self.y + DIRS[k][1] * reach
        return (px >= 0) & (px < self.nx) & (py >= 0) & (py < self.ny), (px, py)

    def tell(self, sem, reach):
        for k in range(8):
            exists, peer = self.far(k, reach)

            @pl.when(exists)
            def _():
                pl.semaphore_signal(sem, inc=1, device_id=peer, device_id_type=MESH)

    def hear(self, sem, reach):
        count = 0
        for k in range(8):
            count = count + self.far(k, reach)[0].astype(jnp.int32)
        pl.semaphore_wait(sem, count)

    def greet(self, barrier, ways=range(8)):
        count = 0
        for k in ways:
            count = count + self.there(k).astype(jnp.int32)

            @pl.when(self.there(k))
            def _():
                pl.semaphore_signal(
                    barrier, inc=1, device_id=self.ident(k), device_id_type=MESH
                )

        return count


def halo_cut(k):
    dx, dy = DIRS[k]
    if dx == 0:
        return (slice(0, 8), slice(0, 4 * BLOCK))
    at, wide = (0, 2) if dy == 0 else (max(dy, 0), 1)
    at = (at + 2 * max(dx, 0)) * BLOCK
    return (slice(0, 8), slice(at, at + wide * BLOCK))


def terms_cut(k):
    rows = {-1: slice(0, 8), 0: slice(0, 16), 1: slice(8, 16)}[DIRS[k][0]]
    return (rows, slice(0, BLOCK))


def image_cut(k):
    return (slice(0, 4), slice(0, BLOCK))


def source_of(cell):
    row, col = cell // 4 + 1, cell % 4 + 1
    dx, dy = row // 2 - 1, col // 2 - 1
    return (dx, dy), (row % 2) * 2 + col % 2


def kernel_value(ax, ay, at, bx, by, bt):
    dx, dy = ax - bx, ay - by
    distance = jnp.sqrt(dx * dx + dy * dy)
    inside = jnp.maximum(1.0 - distance, 0.0)
    square = inside * inside
    return square * square * (4.0 * distance + 1.0) * jnp.exp(-jnp.abs(at - bt))


def thirds(x):
    high = x.astype(jnp.bfloat16).astype(jnp.float32)
    rest = x - high
    mid = rest.astype(jnp.bfloat16).astype(jnp.float32)
    return high, mid, rest - mid


def dot(a, b, rhs=0):
    (a1, a2, a3), (b1, b2, b3) = (
        [x.astype(jnp.bfloat16) for x in thirds(y)] for y in (a, b)
    )
    left = jnp.concatenate([a1, a1, a2, a1, a3, a2], axis=1)
    right = jnp.concatenate([b1, b2, b1, b3, b1, b2], axis=rhs)
    return pick(left, right, rhs)


def pick(a, b, rhs=0):
    return lax.dot_general(
        a, b, (((1,), (rhs,)), ((), ())), preferred_element_type=jnp.float32
    )


def iota(shape, axis):
    return lax.broadcasted_iota(jnp.int32, shape, axis)


def blockdiag(x, first):
    return jnp.concatenate([jnp.where(first, x, 0.0), jnp.where(first, 0.0, x)], axis=0)


def whiten(pair):
    f32 = jnp.float32
    lane = iota((8, BLOCK), 1)
    group, column = lane & HALF, lane & (HALF - 1)
    sub = iota((8, BLOCK), 0)

    def take(x, at):
        return jnp.take_along_axis(x, group + at, axis=1)

    def row(x, j):
        return jnp.broadcast_to(x[j : j + 1, :], (8, BLOCK))

    pair = [list(rows) for rows in pair]
    out = [[None] * 8 for _ in pair]
    for p in range(8):
        at = 8 * p
        inside = (column >= at) & (column < at + 8)
        tops = [[take(rows[p], at + j) for j in range(8)] for rows in pair]
        nexts = [[take(rows[p + 1], at + j) for j in range(8)] for rows in pair if p < 7]
        fars = [
            [[take(rows[v], at + j) for j in range(8)] for v in range(p + 2, 8)] for rows in pair
        ]
        ends = []
        for h, rows in enumerate(pair):
            g = tops[h]
            y = jnp.where(inside, (column == at + sub).astype(f32), rows[p])
            follow = jnp.where(inside, 0.0, rows[p + 1]) if p < 7 else None
            pivots, inverses = None, None
            for j in range(8):
                pivot = row(g[j], j)
                inverse = 1.0 / pivot
                pivots = pivot if j == 0 else jnp.where(sub == j, pivot, pivots)
                inverses = inverse if j == 0 else jnp.where(sub == j, inverse, inverses)
                low = jnp.where(sub > j, g[j] * inverse, 0.0)
                across = [row(g[k], j) for k in range(j + 1, 8)]
                here = row(y, j)
                if j < 7:
                    y = y - low * here
                for k in range(j + 1, 8):
                    g[k] = g[k] - low * across[k - j - 1]
                if p < 7:
                    e = nexts[h]
                    low = e[j] * inverse
                    follow = follow - low * here
                    for k in range(j + 1, 8):
                        e[k] = e[k] - low * across[k - j - 1]
            out[h][p] = jnp.where(column < at + 8, y * lax.rsqrt(pivots), 0.0)
            if p < 7:
                rows[p + 1] = follow
            ends.append((g, y, inverses))
        for h, rows in enumerate(pair):
            if p == 7 or p == 6:
                break
            g, y, inverses = ends[h]
            u = y * inverses
            for j in range(7, 0, -1):
                u = u - jnp.where(sub < j, g[j] * inverses, 0.0) * row(u, j)
            spread = [row(u, k) for k in range(8)]
            for v in range(p + 2, 8):
                t = [fars[h][v - p - 2][k] * spread[k] for k in range(8)]
                total = ((t[0] + t[1]) + (t[2] + t[3])) + ((t[4] + t[5]) + (t[6] + t[7]))
                rows[v] = jnp.where(inside, 0.0, rows[v]) - total
    return [jnp.concatenate(rows, axis=0) for rows in out]


def halves(even, odd, c, first):
    tile = slice(c // 2 * BLOCK, (c // 2 + 1) * BLOCK)
    even, odd = even[:, tile], odd[:, tile]
    if c % 2 == 0:
        odd = pltpu.roll(odd, HALF, axis=1)
    else:
        even = pltpu.roll(even, HALF, axis=1)
    return jnp.where(first, even, odd)


def factor(cc, ll, xx, gg, g_ref, first):
    def own_part():
        for h in range(2):
            after = []
            for c in range(3, -1, -1):
                value = ll[h, c, 4 * HALF :]
                if after:
                    left = jnp.concatenate([gg[h, k] for k in after], axis=1)
                    right = jnp.concatenate(
                        [blockdiag(ll[h, c, k * HALF : (k + 1) * HALF], first) for k in after],
                        axis=0,
                    )
                    value = value - dot(left, right)
                gg[h, c] = dot(value, blockdiag(xx[h, c], first))
                after.append(c)

    for c in range(6):
        at, then = c * HALF, (c + 1) * HALF
        tiles = [[cc[h, c, at + 8 * v : at + 8 * v + 8] for v in range(8)] for h in range(2)]
        found = whiten(tiles)
        for h in range(2):
            xx[h, c] = found[h]
        if c == 5:
            break
        spread = [blockdiag(x, first) for x in found]
        for h in range(2):
            left = dot(cc[h, c, then : then + HALF], spread[h], 1)
            ll[h, c, then : then + HALF] = left
            change = dot(left, blockdiag(left, first), 1)
            cc[h, c + 1, then : then + HALF] = cc[h, c + 1, then : then + HALF] - change
        if c < 4:
            after = then + HALF
            for h in range(2):
                ll[h, c, after:] = dot(cc[h, c, after:], spread[h], 1)
            for other in range(c + 1, 6):
                start = other * HALF
                top = after if other == c + 1 else start
                for h in range(2):
                    right = blockdiag(ll[h, c, start : start + HALF], first)
                    change = dot(ll[h, c, top:], right, 1)
                    cc[h, other, top:] = cc[h, other, top:] - change
        if c == 3:
            own_part()
    for h in range(2):
        x4, x5 = xx[h, 4], xx[h, 5]
        l54 = ll[h, 4, 5 * HALF :]
        right = jnp.concatenate([blockdiag(gg[h, c, 0:HALF], first) for c in range(4)], axis=1)
        upper = -dot(x4, right)
        upper = [upper[:, c * BLOCK : (c + 1) * BLOCK] for c in range(4)] + [x4]
        right = jnp.concatenate([blockdiag(x, first) for x in upper], axis=1)
        mixed = dot(l54, right)
        mixed = [mixed[:, c * BLOCK : (c + 1) * BLOCK] for c in range(5)]
        mixed = [mixed[c] + gg[h, c, HALF:] for c in range(4)] + [mixed[4]]
        right = jnp.concatenate([blockdiag(x, first) for x in mixed], axis=1)
        lower = -dot(x5, right)
        lower = [lower[:, c * BLOCK : (c + 1) * BLOCK] for c in range(5)] + [x5]
        upper = upper + [jnp.zeros_like(x5)]
        for c in range(6):
            g_ref[h, c, 0:HALF] = upper[c]
            g_ref[h, c, HALF:] = lower[c]


def solve_kernel(nx, ny, *refs):
    (coords, listed_hbm, noise_hbm, obs_hbm, mean_ref, res_ref) = refs[:6]
    (own, land, listed_ref, f_ref, hot, cc, ll, xx, gg, g_ref, seen, k_ref) = refs[6:18]
    (res, terms, terms_in, total, image, image_in, sums, sums_y, sums_x) = refs[18:27]
    (load, send_h, recv_h, send_t, recv_t, send_i, recv_i) = refs[27:34]
    (send_y, recv_y, send_x, recv_x, known) = refs[34:]
    f32 = jnp.float32
    links = Links(nx, ny)
    gx, gy = links.x, links.y
    direct = max(nx, ny) <= 8
    barrier = pltpu.get_barrier_semaphore()
    if direct:
        me, size = gx * ny + gy, nx * ny
        places = [lax.rem(me + off, size) for off in range(1, size)]
        line_y = [(lax.div(at, ny), lax.rem(at, ny)) for at in places]
        line_x, greeted = [], links.greet(barrier)
    else:
        me, size = gy, ny
        greeted = links.greet(barrier, [k for k in range(8) if 0 not in DIRS[k]]) + nx + ny - 2
        line_y = [(gx, lax.rem(gy + off, ny)) for off in range(1, ny)]
        line_x = [(lax.rem(gx + off, nx), gy) for off in range(1, nx)]
    for peer in [] if direct else line_y + line_x:
        pl.semaphore_signal(barrier, inc=1, device_id=peer, device_id_type=MESH)
    loads = [
        pltpu.make_async_copy(coords.at[axis, 0], own.at[axis : axis + 1], load.at[axis])
        for axis in range(3)
    ]
    loads.append(pltpu.make_async_copy(noise_hbm, own.at[3:4], load.at[3]))
    loads.append(pltpu.make_async_copy(obs_hbm, own.at[4:5], load.at[4]))
    loads.append(pltpu.make_async_copy(listed_hbm.at[0, 0], listed_ref, load.at[5]))
    for copy in loads:
        copy.start()
    own[5:8] = jnp.zeros((3, own.shape[1]), f32)
    image[...] = jnp.zeros_like(image)
    for copy in loads:
        copy.wait()
    pl.semaphore_wait(barrier, greeted)
    reaches = [1 << r for r in range(3)] if direct else []
    if direct:
        links.tell(known.at[0], 1)

    def widen(r):
        if direct:
            links.hear(known.at[r], reaches[r])
            if r < 2:
                links.tell(known.at[r + 1], reaches[r + 1])

    halo = (own, land, send_h, recv_h, halo_cut)
    links.start(*halo)

    lane = iota((1, BLOCK), 1)
    front = lane < HALF
    listed = listed_ref[...]
    slot, within = listed >> 9, listed & 511
    third = (slot * 11) >> 5
    row = third * 2 + (within >> 8) - 1
    col = (slot - 3 * third) * 2 + ((within >> 7) & 1) - 1
    index = jnp.where(listed >= 0, (row * 4 + col) * BLOCK + (within & 127), -1)
    idx = index.astype(f32)
    idx_t = jnp.concatenate([idx, idx], axis=0).T
    lane_f = lane.astype(f32)
    away = []
    for h in range(2):
        for s in range(2):
            chosen = idx_t[:, 2 * h + s : 2 * h + s + 1]
            for q, cell in enumerate(others(2 * h + s)):
                same = (chosen == lane_f + float(cell * BLOCK)).astype(f32).astype(jnp.bfloat16)
                for c in range(4):
                    at = c * BLOCK + s * HALF
                    part = same[c * HALF : (c + 1) * HALF]
                    hot[h, at : at + HALF, q * BLOCK : (q + 1) * BLOCK] = part
        even, odd = idx[2 * h : 2 * h + 1], idx[2 * h + 1 : 2 * h + 2]
        dead = jnp.concatenate([halves(even, odd, c, front) for c in range(4)], axis=1) < 0.0
        away.append(jnp.where(dead, 1000.0 * (iota((1, 4 * BLOCK), 1) + 1).astype(f32), 0.0))

    links.finish(*halo)
    for cell in range(16):
        way, inner = source_of(cell)
        part = slice(inner * BLOCK, (inner + 1) * BLOCK)
        value = own[:, part] if way == (0, 0) else land[DIRS.index(way), :, part]
        f_ref[:, cell * BLOCK : (cell + 1) * BLOCK] = value
    for cell in range(16):
        res[cell : cell + 1, :] = f_ref[4:5, cell * BLOCK : (cell + 1) * BLOCK]
    noise = [f_ref[3:4, c * BLOCK : (c + 1) * BLOCK] for c in OWN]

    def gather(h, even, odd):
        n = even.shape[0]
        rows = [*thirds(even), *thirds(odd)]
        fill = (-6 * n) % 16
        if fill:
            rows.append(jnp.zeros((fill, even.shape[1]), f32))
        found = pick(jnp.concatenate(rows, axis=0).astype(jnp.bfloat16), hot[h], 1)
        even = found[0:n] + found[n : 2 * n] + found[2 * n : 3 * n]
        odd = found[3 * n : 4 * n] + found[4 * n : 5 * n] + found[5 * n : 6 * n]
        return jnp.where((iota((1, 4 * BLOCK), 1) & HALF) == 0, even, odd)

    for h in range(2):
        near = [
            jnp.concatenate(
                [f_ref[:, cell * BLOCK : (cell + 1) * BLOCK] for cell in others(2 * h + s)], axis=1
            )
            for s in range(2)
        ]
        x = gather(h, *near)
        seen[h, 0:4] = jnp.concatenate(
            [x[4:5, c * BLOCK : (c + 1) * BLOCK] for c in range(4)], axis=0
        )
        x = jnp.where(iota((8, 4 * BLOCK), 0) == 0, x + away[h], x)
        mine = [f_ref[:, OWN[2 * h + s] * BLOCK : (OWN[2 * h + s] + 1) * BLOCK] for s in range(2)]
        x = jnp.concatenate([x] + [halves(*mine, c, front) for c in range(2)], axis=1)
        seen[h, 4:6] = jnp.concatenate(
            [x[4:5, c * BLOCK : (c + 1) * BLOCK] for c in range(4, 6)], axis=0
        )
        t = x.T
        even_t, odd_t = (
            jnp.concatenate(
                [t[c * BLOCK + s * HALF : c * BLOCK + (s + 1) * HALF] for c in range(6)], axis=0
            )
            for s in range(2)
        )
        down = [jnp.where(front, even_t[:, a : a + 1], odd_t[:, a : a + 1]) for a in range(3)]
        for c in range(6):
            o = x[:, c * BLOCK : (c + 1) * BLOCK]
            at = c * HALF
            kern = kernel_value(*[d[at:] for d in down], o[0:1], o[1:2], o[2:3])
            diagonal = iota((HALF, BLOCK), 0) == (iota((HALF, BLOCK), 1) & (HALF - 1))
            cc[h, c, at : at + HALF] = kern[:HALF] + jnp.where(diagonal, o[3:4], 0.0)
            if c < 5:
                cc[h, c, at + HALF :] = kern[HALF:]
    widen(0)
    factor(cc, ll, xx, gg, g_ref, front)
    widen(1)

    def precondition(step):
        out = [jnp.zeros((1, BLOCK), f32) for _ in range(16)]
        for h in range(2):
            ends = (2 * h, 2 * h + 1)
            if step == 0:
                v = [seen[h, c : c + 1, :] for c in range(6)]
            else:
                near = [jnp.concatenate([res[c : c + 1] for c in others(b)], axis=1) for b in ends]
                found = gather(h, *near)
                v = [found[:, c * BLOCK : (c + 1) * BLOCK] for c in range(4)]
                mine = [res[OWN[b] : OWN[b] + 1] for b in ends]
                v = v + [halves(*mine, c, front) for c in range(2)]
            acc = g_ref[h, 0] * v[0]
            for c in range(1, 6):
                acc = acc + g_ref[h, c] * v[c]
            even = jnp.sum(jnp.where(front, acc, 0.0), axis=1, keepdims=True)
            odd = jnp.sum(jnp.where(front, 0.0, acc), axis=1, keepdims=True)
            w = jnp.where(front, even, odd)
            t = [jnp.sum(g_ref[h, c] * w, axis=0, keepdims=True) for c in range(6)]
            wide = jnp.concatenate(t[0:4], axis=1)
            half = (iota((1, 4 * BLOCK), 1) & HALF) == 0
            rows = [*thirds(jnp.where(half, wide, 0.0)), *thirds(jnp.where(half, 0.0, wide))]
            rows.append(jnp.zeros((10, 4 * BLOCK), f32))
            found = pick(jnp.concatenate(rows, axis=0).astype(jnp.bfloat16), hot[h])
            turned = [pltpu.roll(x, HALF, axis=1) for x in t[4:6]]
            kept = [jnp.where(front, t[4], turned[1]), jnp.where(front, turned[0], t[5])]
            for s, b in enumerate(ends):
                value = found[3 * s : 3 * s + 1] + found[3 * s + 1 : 3 * s + 2]
                value = value + found[3 * s + 2 : 3 * s + 3]
                for q, cell in enumerate(others(b)):
                    out[cell] = out[cell] + value[:, q * BLOCK : (q + 1) * BLOCK]
                out[OWN[b]] = out[OWN[b]] + kept[s]
        for cell in range(16):
            terms[step, cell : cell + 1, :] = out[cell]

    def fill_kernel():
        parts = [f_ref[:, cell * BLOCK : (cell + 1) * BLOCK] for cell in range(16)]
        turned = [parts[c].T for c in OWN]
        for b in range(4):
            t = turned[b]
            for q, cell in enumerate(around(b)):
                o = parts[cell]
                kern = kernel_value(t[:, 0:1], t[:, 1:2], t[:, 2:3], o[0:1], o[1:2], o[2:3])
                k_ref[b, q] = kern

    def exchange_terms(step):
        args = (terms.at[step], terms_in.at[step], send_t.at[step], recv_t.at[step], terms_cut)
        links.start(*args)
        if step == 0:
            fill_kernel()
        links.finish(*args)
        for cell in range(16):
            r, c = cell // 4, cell % 4
            value = terms[step, cell : cell + 1, :]
            for k, (dx, dy) in enumerate(DIRS):
                rr, cc = r - 2 * dx, c - 2 * dy
                if 0 <= rr < 4 and 0 <= cc < 4:
                    at = rr * 4 + cc
                    value = value + terms_in[step, k, at : at + 1, :]
            if step == 1:
                value = value - total[0, cell : cell + 1, :]
            total[step, cell : cell + 1, :] = value

    def operate(step):
        diagonal = iota((BLOCK, BLOCK), 0) == iota((BLOCK, BLOCK), 1)
        for b in range(4):
            acc = jnp.zeros((BLOCK, BLOCK), f32)
            for q, cell in enumerate(around(b)):
                acc = acc + k_ref[b, q] * total[step, cell : cell + 1, :]
            down = jnp.sum(acc, axis=1, keepdims=True)
            value = jnp.sum(jnp.where(diagonal, down, 0.0), axis=0, keepdims=True)
            value = value + noise[b] * total[step, OWN[b] : OWN[b] + 1, :]
            image[step, b : b + 1, :] = value

    def line_copy(src, buf, send, recv, peer, at, off):
        return pltpu.make_async_remote_copy(
            src_ref=src,
            dst_ref=buf.at[at],
            send_sem=send.at[off],
            recv_sem=recv.at[off],
            device_id=peer,
            device_id_type=MESH,
        )

    def reduce_line(src, buf, send, recv, peers, me, size):
        copies = [line_copy(src, buf, send, recv, p, me, o) for o, p in enumerate(peers)]
        for copy in copies:
            copy.start()
        buf[me] = src[...]
        for copy in copies:
            copy.wait()
        value = buf[0]
        for at in range(1, size):
            value = value + buf[at]
        return value

    def reduce_all(rows):
        lanes = iota((1, BLOCK), 1)
        packed = jnp.zeros((1, BLOCK), jnp.float32)
        for at, row in enumerate(rows):
            packed = packed + jnp.where(lanes == at, jnp.sum(row, axis=1, keepdims=True), 0.0)
        sums[0] = packed
        value = reduce_line(sums.at[0], sums_y, send_y, recv_y, line_y, me, size)
        if not direct:
            sums[1] = value
            value = reduce_line(sums.at[1], sums_x, send_x, recv_x, line_x, gx, nx)
        return [
            jnp.sum(jnp.where(lanes == at, value, 0.0), axis=1, keepdims=True)
            for at in range(len(rows))
        ]

    def across(left, right):
        value = left[0] * right[0]
        for a, b in zip(left[1:], right[1:]):
            value = value + a * b
        return value

    def mine(ref, step):
        return [ref[step, c : c + 1, :] for c in OWN]

    precondition(0)
    exchange_terms(0)
    operate(0)
    args = (image.at[0], image_in, send_i, recv_i, image_cut)
    links.start(*args)
    first = mine(total, 0)
    along = [image[0, b : b + 1, :] for b in range(4)]
    start = [res[c : c + 1, :] for c in OWN]
    links.finish(*args)
    for cell in range(16):
        way, inner = source_of(cell)
        if way == (0, 0):
            value = image[0, inner : inner + 1, :]
        else:
            value = image_in[DIRS.index(way), inner : inner + 1, :]
        res[cell : cell + 1, :] = value
    precondition(1)
    widen(2)
    exchange_terms(1)
    operate(1)
    second = mine(total, 1)
    along2 = [image[1, b : b + 1, :] for b in range(4)]
    base, extra, cross, curve = reduce_all(
        [
            across(first, along),
            across([s - a for s, a in zip(start, along)], first),
            across(along, second),
            across(second, along2),
        ]
    )
    share = extra / base
    alpha = 1.0 + share
    kappa = alpha * cross / base
    alpha2 = (share + kappa) * base / (alpha * (curve - cross * cross / base))
    for b in range(4):
        solved = alpha * first[b] + alpha2 * (kappa * first[b] - alpha * second[b])
        part = slice(b * BLOCK, (b + 1) * BLOCK)
        mean_ref[:, part] = start[b] - noise[b] * solved
        left = start[b] - alpha * along[b]
        res_ref[:, part] = left - alpha2 * (kappa * along[b] - alpha * along2[b])


def local(nx, ny, coords, neighbours, noise_var, observations):
    tile = observations.shape[2]
    line = nx * ny if max(nx, ny) <= 8 else ny
    f32 = jnp.float32
    vmem = pl.BlockSpec(memory_space=pltpu.VMEM)
    dma = pltpu.SemaphoreType.DMA
    whole = pl.BlockSpec(memory_space=pl.ANY)
    mean, residual = pl.pallas_call(
        functools.partial(solve_kernel, nx, ny),
        out_shape=(jax.ShapeDtypeStruct((1, tile), f32),) * 2,
        in_specs=[whole] * 4,
        out_specs=[vmem] * 2,
        scratch_shapes=[
            pltpu.VMEM((8, tile), f32),
            pltpu.VMEM((8, 8, tile), f32),
            pltpu.VMEM((4, NEIGH), jnp.int32),
            pltpu.VMEM((8, 16 * BLOCK), f32),
            pltpu.VMEM((2, 4 * BLOCK, 8 * BLOCK), jnp.bfloat16),
            pltpu.VMEM((2, 6, 6 * HALF, BLOCK), f32),
            pltpu.VMEM((2, 5, 6 * HALF, BLOCK), f32),
            pltpu.VMEM((2, 6, HALF, BLOCK), f32),
            pltpu.VMEM((2, 4, BLOCK, BLOCK), f32),
            pltpu.VMEM((2, 6, BLOCK, BLOCK), f32),
            pltpu.VMEM((2, 8, BLOCK), f32),
            pltpu.VMEM((4, 9, BLOCK, BLOCK), f32),
            pltpu.VMEM((16, BLOCK), f32),
            pltpu.VMEM((2, 16, BLOCK), f32),
            pltpu.VMEM((2, 8, 16, BLOCK), f32),
            pltpu.VMEM((2, 16, BLOCK), f32),
            pltpu.VMEM((2, 8, BLOCK), f32),
            pltpu.VMEM((8, 8, BLOCK), f32),
            pltpu.VMEM((2, 1, BLOCK), f32),
            pltpu.VMEM((line, 1, BLOCK), f32),
            pltpu.VMEM((nx, 1, BLOCK), f32),
            dma((6,)),
            dma((8,)),
            dma((8,)),
            dma((2, 8)),
            dma((2, 8)),
            dma((8,)),
            dma((8,)),
            dma((line,)),
            dma((line,)),
            dma((nx,)),
            dma((nx,)),
            pltpu.SemaphoreType.REGULAR((3,)),
        ],
        compiler_params=pltpu.CompilerParams(
            collective_id=0, has_side_effects=True, vmem_limit_bytes=60 << 20
        ),
        name="solve",
    )(coords, neighbours, noise_var.reshape(1, tile), observations.reshape(1, tile))
    return (mean.reshape(observations.shape), residual.reshape(observations.shape))


def solution(mesh):
    in_specs = (
        P(None, "gx", "gy", None),
        P("gx", "gy", None, None),
        P("gx", "gy", None),
        P("gx", "gy", None),
    )
    out_specs = (P("gx", "gy", None), P("gx", "gy", None))
    body = functools.partial(local, mesh.shape["gx"], mesh.shape["gy"])
    return jax.shard_map(body, mesh=mesh, in_specs=in_specs, out_specs=out_specs, check_vma=False)
```

```python
import functools

import jax
import jax.numpy as jnp
from jax import lax
from jax.experimental import pallas as pl
from jax.experimental.pallas import tpu as pltpu
from jax.sharding import PartitionSpec as P

MESH = pl.DeviceIdType.MESH
BLOCK = 128
NEIGH = 256
HALF = 64
HIGH = lax.Precision.HIGHEST
DIRS = [(dx, dy) for dx in (-1, 0, 1) for dy in (-1, 0, 1) if (dx, dy) != (0, 0)]
OWN = [5, 6, 9, 10]
FAR_FIRST = [0, 2, 5, 7, 1, 6, 3, 4]


def around(b):
    r, c = 1 + b // 2, 1 + b % 2
    return [(r - 1 + q // 3) * 4 + c - 1 + q % 3 for q in range(9)]


def others(b):
    return [cell for q, cell in enumerate(around(b)) if q != 4]


class Links:
    def __init__(self, nx, ny):
        self.nx, self.ny = nx, ny
        self.x, self.y = lax.axis_index("gx"), lax.axis_index("gy")

    def there(self, k):
        dx, dy = DIRS[k]
        px, py = self.x + dx, self.y + dy
        return (px >= 0) & (px < self.nx) & (py >= 0) & (py < self.ny)

    def ident(self, k):
        return (self.x + DIRS[k][0], self.y + DIRS[k][1])

    def copy(self, k, slot, src, dst, send, recv, part):
        return pltpu.make_async_remote_copy(
            src_ref=src.at[part],
            dst_ref=dst.at[(slot, *part)],
            send_sem=send.at[k],
            recv_sem=recv.at[slot],
            device_id=self.ident(k),
            device_id_type=MESH,
        )

    def start(self, src, dst, send, recv, cut):
        for k in FAR_FIRST:

            @pl.when(self.there(k))
            def _():
                self.copy(k, 7 - k, src, dst, send, recv, cut(k)).start()

        for k in range(8):

            @pl.when(jnp.logical_not(self.there(k)))
            def _():
                dst[k] = jnp.zeros(dst.shape[1:], dst.dtype)

    def finish(self, src, dst, send, recv, cut):
        for k in range(8):

            @pl.when(self.there(k))
            def _():
                self.copy(k, k, src, dst, send, recv, cut(k)).wait_send()
                self.copy(k, k, src, dst, send, recv, cut(7 - k)).wait_recv()

    def far(self, k, reach):
        px, py = self.x + DIRS[k][0] * reach, self.y + DIRS[k][1] * reach
        return (px >= 0) & (px < self.nx) & (py >= 0) & (py < self.ny), (px, py)

    def tell(self, sem, reach):
        for k in range(8):
            exists, peer = self.far(k, reach)

            @pl.when(exists)
            def _():
                pl.semaphore_signal(sem, inc=1, device_id=peer, device_id_type=MESH)

    def hear(self, sem, reach):
        count = 0
        for k in range(8):
            count = count + self.far(k, reach)[0].astype(jnp.int32)
        pl.semaphore_wait(sem, count)

    def greet(self, barrier, ways=range(8)):
        count = 0
        for k in ways:
            count = count + self.there(k).astype(jnp.int32)

            @pl.when(self.there(k))
            def _():
                pl.semaphore_signal(
                    barrier, inc=1, device_id=self.ident(k), device_id_type=MESH
                )

        return count


def halo_cut(k):
    dx, dy = DIRS[k]
    if dx == 0:
        return (slice(0, 8), slice(0, 4 * BLOCK))
    at, wide = (0, 2) if dy == 0 else (max(dy, 0), 1)
    at = (at + 2 * max(dx, 0)) * BLOCK
    return (slice(0, 8), slice(at, at + wide * BLOCK))


def terms_cut(k):
    rows = {-1: slice(0, 8), 0: slice(0, 16), 1: slice(8, 16)}[DIRS[k][0]]
    return (rows, slice(0, BLOCK))


def image_cut(k):
    return (slice(0, 4), slice(0, BLOCK))


def source_of(cell):
    row, col = cell // 4 + 1, cell % 4 + 1
    dx, dy = row // 2 - 1, col // 2 - 1
    return (dx, dy), (row % 2) * 2 + col % 2


def kernel_value(ax, ay, at, bx, by, bt):
    dx, dy = ax - bx, ay - by
    distance = jnp.sqrt(dx * dx + dy * dy)
    inside = jnp.maximum(1.0 - distance, 0.0)
    square = inside * inside
    return square * square * (4.0 * distance + 1.0) * jnp.exp(-jnp.abs(at - bt))


def thirds(x):
    high = x.astype(jnp.bfloat16).astype(jnp.float32)
    rest = x - high
    mid = rest.astype(jnp.bfloat16).astype(jnp.float32)
    return high, mid, rest - mid


def dot(a, b, rhs=0):
    (a1, a2, a3), (b1, b2, b3) = (
        [x.astype(jnp.bfloat16) for x in thirds(y)] for y in (a, b)
    )
    left = jnp.concatenate([a1, a1, a2, a1, a3, a2], axis=1)
    right = jnp.concatenate([b1, b2, b1, b3, b1, b2], axis=rhs)
    return pick(left, right, rhs)


def pick(a, b, rhs=0):
    return lax.dot_general(
        a, b, (((1,), (rhs,)), ((), ())), preferred_element_type=jnp.float32
    )


def iota(shape, axis):
    return lax.broadcasted_iota(jnp.int32, shape, axis)


def blockdiag(x, first):
    return jnp.concatenate([jnp.where(first, x, 0.0), jnp.where(first, 0.0, x)], axis=0)


def whiten(pair):
    f32 = jnp.float32
    lane = iota((8, BLOCK), 1)
    group, column = lane & HALF, lane & (HALF - 1)
    sub = iota((8, BLOCK), 0)

    def take(x, at):
        return jnp.take_along_axis(x, group + at, axis=1)

    def row(x, j):
        return jnp.broadcast_to(x[j : j + 1, :], (8, BLOCK))

    pair = [list(rows) for rows in pair]
    out = [[None] * 8 for _ in pair]
    for p in range(8):
        at = 8 * p
        inside = (column >= at) & (column < at + 8)
        tops = [[take(rows[p], at + j) for j in range(8)] for rows in pair]
        nexts = [[take(rows[p + 1], at + j) for j in range(8)] for rows in pair if p < 7]
        fars = [
            [[take(rows[v], at + j) for j in range(8)] for v in range(p + 2, 8)] for rows in pair
        ]
        ends = []
        for h, rows in enumerate(pair):
            g = tops[h]
            y = jnp.where(inside, (column == at + sub).astype(f32), rows[p])
            follow = jnp.where(inside, 0.0, rows[p + 1]) if p < 7 else None
            pivots, inverses = None, None
            for j in range(8):
                pivot = row(g[j], j)
                inverse = 1.0 / pivot
                pivots = pivot if j == 0 else jnp.where(sub == j, pivot, pivots)
                inverses = inverse if j == 0 else jnp.where(sub == j, inverse, inverses)
                low = jnp.where(sub > j, g[j] * inverse, 0.0)
                across = [row(g[k], j) for k in range(j + 1, 8)]
                here = row(y, j)
                if j < 7:
                    y = y - low * here
                for k in range(j + 1, 8):
                    g[k] = g[k] - low * across[k - j - 1]
                if p < 7:
                    e = nexts[h]
                    low = e[j] * inverse
                    follow = follow - low * here
                    for k in range(j + 1, 8):
                        e[k] = e[k] - low * across[k - j - 1]
            out[h][p] = jnp.where(column < at + 8, y * lax.rsqrt(pivots), 0.0)
            if p < 7:
                rows[p + 1] = follow
            ends.append((g, y, inverses))
        for h, rows in enumerate(pair):
            if p == 7 or p == 6:
                break
            g, y, inverses = ends[h]
            u = y * inverses
            for j in range(7, 0, -1):
                u = u - jnp.where(sub < j, g[j] * inverses, 0.0) * row(u, j)
            spread = [row(u, k) for k in range(8)]
            for v in range(p + 2, 8):
                t = [fars[h][v - p - 2][k] * spread[k] for k in range(8)]
                total = ((t[0] + t[1]) + (t[2] + t[3])) + ((t[4] + t[5]) + (t[6] + t[7]))
                rows[v] = jnp.where(inside, 0.0, rows[v]) - total
    return [jnp.concatenate(rows, axis=0) for rows in out]


def halves(even, odd, c, first):
    tile = slice(c // 2 * BLOCK, (c // 2 + 1) * BLOCK)
    even, odd = even[:, tile], odd[:, tile]
    if c % 2 == 0:
        odd = pltpu.roll(odd, HALF, axis=1)
    else:
        even = pltpu.roll(even, HALF, axis=1)
    return jnp.where(first, even, odd)


def factor(cc, ll, xx, gg, g_ref, first):
    def own_part():
        for h in range(2):
            after = []
            for c in range(3, -1, -1):
                value = ll[h, c, 4 * HALF :]
                if after:
                    left = jnp.concatenate([gg[h, k] for k in after], axis=1)
                    right = jnp.concatenate(
                        [blockdiag(ll[h, c, k * HALF : (k + 1) * HALF], first) for k in after],
                        axis=0,
                    )
                    value = value - dot(left, right)
                gg[h, c] = dot(value, blockdiag(xx[h, c], first))
                after.append(c)

    for c in range(6):
        at, then = c * HALF, (c + 1) * HALF
        tiles = [[cc[h, c, at + 8 * v : at + 8 * v + 8] for v in range(8)] for h in range(2)]
        found = whiten(tiles)
        for h in range(2):
            xx[h, c] = found[h]
        if c == 5:
            break
        spread = [blockdiag(x, first) for x in found]
        for h in range(2):
            left = dot(cc[h, c, then : then + HALF], spread[h], 1)
            ll[h, c, then : then + HALF] = left
            change = dot(left, blockdiag(left, first), 1)
            cc[h, c + 1, then : then + HALF] = cc[h, c + 1, then : then + HALF] - change
        if c < 4:
            after = then + HALF
            for h in range(2):
                ll[h, c, after:] = dot(cc[h, c, after:], spread[h], 1)
            for other in range(c + 1, 6):
                start = other * HALF
                top = after if other == c + 1 else start
                for h in range(2):
                    right = blockdiag(ll[h, c, start : start + HALF], first)
                    change = dot(ll[h, c, top:], right, 1)
                    cc[h, other, top:] = cc[h, other, top:] - change
        if c == 3:
            own_part()
    for h in range(2):
        x4, x5 = xx[h, 4], xx[h, 5]
        l54 = ll[h, 4, 5 * HALF :]
        right = jnp.concatenate([blockdiag(gg[h, c, 0:HALF], first) for c in range(4)], axis=1)
        upper = -dot(x4, right)
        upper = [upper[:, c * BLOCK : (c + 1) * BLOCK] for c in range(4)] + [x4]
        right = jnp.concatenate([blockdiag(x, first) for x in upper], axis=1)
        mixed = dot(l54, right)
        mixed = [mixed[:, c * BLOCK : (c + 1) * BLOCK] for c in range(5)]
        mixed = [mixed[c] + gg[h, c, HALF:] for c in range(4)] + [mixed[4]]
        right = jnp.concatenate([blockdiag(x, first) for x in mixed], axis=1)
        lower = -dot(x5, right)
        lower = [lower[:, c * BLOCK : (c + 1) * BLOCK] for c in range(5)] + [x5]
        upper = upper + [jnp.zeros_like(x5)]
        for c in range(6):
            g_ref[h, c, 0:HALF] = upper[c]
            g_ref[h, c, HALF:] = lower[c]


def solve_kernel(nx, ny, *refs):
    (coords, listed_hbm, noise_hbm, obs_hbm, mean_ref, res_ref) = refs[:6]
    (own, land, listed_ref, f_ref, hot, cc, ll, xx, gg, g_ref, seen, k_ref) = refs[6:18]
    (res, terms, terms_in, total, image, image_in, sums, sums_y, sums_x) = refs[18:27]
    (load, send_h, recv_h, send_t, recv_t, send_i, recv_i) = refs[27:34]
    (send_y, recv_y, send_x, recv_x, known) = refs[34:]
    f32 = jnp.float32
    links = Links(nx, ny)
    gx, gy = links.x, links.y
    direct = max(nx, ny) <= 8
    barrier = pltpu.get_barrier_semaphore()
    if direct:
        me, size = gx * ny + gy, nx * ny
        places = [lax.rem(me + off, size) for off in range(1, size)]
        line_y = [(lax.div(at, ny), lax.rem(at, ny)) for at in places]
        line_x, greeted = [], links.greet(barrier)
    else:
        me, size = gy, ny
        greeted = links.greet(barrier, [k for k in range(8) if 0 not in DIRS[k]]) + nx + ny - 2
        line_y = [(gx, lax.rem(gy + off, ny)) for off in range(1, ny)]
        line_x = [(lax.rem(gx + off, nx), gy) for off in range(1, nx)]
    for peer in [] if direct else line_y + line_x:
        pl.semaphore_signal(barrier, inc=1, device_id=peer, device_id_type=MESH)
    loads = [
        pltpu.make_async_copy(coords.at[axis, 0], own.at[axis : axis + 1], load.at[axis])
        for axis in range(3)
    ]
    loads.append(pltpu.make_async_copy(noise_hbm, own.at[3:4], load.at[3]))
    loads.append(pltpu.make_async_copy(obs_hbm, own.at[4:5], load.at[4]))
    loads.append(pltpu.make_async_copy(listed_hbm.at[0, 0], listed_ref, load.at[5]))
    for copy in loads:
        copy.start()
    own[5:8] = jnp.zeros((3, own.shape[1]), f32)
    image[...] = jnp.zeros_like(image)
    for copy in loads:
        copy.wait()
    pl.semaphore_wait(barrier, greeted)
    reaches = [1 << r for r in range(3)] if direct else []
    if direct:
        links.tell(known.at[0], 1)

    def widen(r):
        if direct:
            links.hear(known.at[r], reaches[r])
            if r < 2:
                links.tell(known.at[r + 1], reaches[r + 1])

    halo = (own, land, send_h, recv_h, halo_cut)
    links.start(*halo)

    lane = iota((1, BLOCK), 1)
    front = lane < HALF
    listed = listed_ref[...]
    slot, within = listed >> 9, listed & 511
    third = (slot * 11) >> 5
    row = third * 2 + (within >> 8) - 1
    col = (slot - 3 * third) * 2 + ((within >> 7) & 1) - 1
    index = jnp.where(listed >= 0, (row * 4 + col) * BLOCK + (within & 127), -1)
    idx = index.astype(f32)
    idx_t = jnp.concatenate([idx, idx], axis=0).T
    lane_f = lane.astype(f32)
    away = []
    for h in range(2):
        for s in range(2):
            chosen = idx_t[:, 2 * h + s : 2 * h + s + 1]
            for q, cell in enumerate(others(2 * h + s)):
                same = (chosen == lane_f + float(cell * BLOCK)).astype(f32).astype(jnp.bfloat16)
                for c in range(4):
                    at = c * BLOCK + s * HALF
                    part = same[c * HALF : (c + 1) * HALF]
                    hot[h, at : at + HALF, q * BLOCK : (q + 1) * BLOCK] = part
        even, odd = idx[2 * h : 2 * h + 1], idx[2 * h + 1 : 2 * h + 2]
        dead = jnp.concatenate([halves(even, odd, c, front) for c in range(4)], axis=1) < 0.0
        away.append(jnp.where(dead, 1000.0 * (iota((1, 4 * BLOCK), 1) + 1).astype(f32), 0.0))

    widen(0)
    links.finish(*halo)
    for cell in range(16):
        way, inner = source_of(cell)
        part = slice(inner * BLOCK, (inner + 1) * BLOCK)
        value = own[:, part] if way == (0, 0) else land[DIRS.index(way), :, part]
        f_ref[:, cell * BLOCK : (cell + 1) * BLOCK] = value
    for cell in range(16):
        res[cell : cell + 1, :] = f_ref[4:5, cell * BLOCK : (cell + 1) * BLOCK]
    noise = [f_ref[3:4, c * BLOCK : (c + 1) * BLOCK] for c in OWN]

    def gather(h, even, odd):
        n = even.shape[0]
        rows = [*thirds(even), *thirds(odd)]
        fill = (-6 * n) % 16
        if fill:
            rows.append(jnp.zeros((fill, even.shape[1]), f32))
        found = pick(jnp.concatenate(rows, axis=0).astype(jnp.bfloat16), hot[h], 1)
        even = found[0:n] + found[n : 2 * n] + found[2 * n : 3 * n]
        odd = found[3 * n : 4 * n] + found[4 * n : 5 * n] + found[5 * n : 6 * n]
        return jnp.where((iota((1, 4 * BLOCK), 1) & HALF) == 0, even, odd)

    for h in range(2):
        near = [
            jnp.concatenate(
                [f_ref[:, cell * BLOCK : (cell + 1) * BLOCK] for cell in others(2 * h + s)], axis=1
            )
            for s in range(2)
        ]
        x = gather(h, *near)
        seen[h, 0:4] = jnp.concatenate(
            [x[4:5, c * BLOCK : (c + 1) * BLOCK] for c in range(4)], axis=0
        )
        x = jnp.where(iota((8, 4 * BLOCK), 0) == 0, x + away[h], x)
        mine = [f_ref[:, OWN[2 * h + s] * BLOCK : (OWN[2 * h + s] + 1) * BLOCK] for s in range(2)]
        x = jnp.concatenate([x] + [halves(*mine, c, front) for c in range(2)], axis=1)
        seen[h, 4:6] = jnp.concatenate(
            [x[4:5, c * BLOCK : (c + 1) * BLOCK] for c in range(4, 6)], axis=0
        )
        t = x.T
        even_t, odd_t = (
            jnp.concatenate(
                [t[c * BLOCK + s * HALF : c * BLOCK + (s + 1) * HALF] for c in range(6)], axis=0
            )
            for s in range(2)
        )
        down = [jnp.where(front, even_t[:, a : a + 1], odd_t[:, a : a + 1]) for a in range(3)]
        for c in range(6):
            o = x[:, c * BLOCK : (c + 1) * BLOCK]
            at = c * HALF
            kern = kernel_value(*[d[at:] for d in down], o[0:1], o[1:2], o[2:3])
            diagonal = iota((HALF, BLOCK), 0) == (iota((HALF, BLOCK), 1) & (HALF - 1))
            cc[h, c, at : at + HALF] = kern[:HALF] + jnp.where(diagonal, o[3:4], 0.0)
            if c < 5:
                cc[h, c, at + HALF :] = kern[HALF:]
    factor(cc, ll, xx, gg, g_ref, front)

    def precondition(step):
        out = [jnp.zeros((1, BLOCK), f32) for _ in range(16)]
        for h in range(2):
            ends = (2 * h, 2 * h + 1)
            if step == 0:
                v = [seen[h, c : c + 1, :] for c in range(6)]
            else:
                near = [jnp.concatenate([res[c : c + 1] for c in others(b)], axis=1) for b in ends]
                found = gather(h, *near)
                v = [found[:, c * BLOCK : (c + 1) * BLOCK] for c in range(4)]
                mine = [res[OWN[b] : OWN[b] + 1] for b in ends]
                v = v + [halves(*mine, c, front) for c in range(2)]
            acc = g_ref[h, 0] * v[0]
            for c in range(1, 6):
                acc = acc + g_ref[h, c] * v[c]
            even = jnp.sum(jnp.where(front, acc, 0.0), axis=1, keepdims=True)
            odd = jnp.sum(jnp.where(front, 0.0, acc), axis=1, keepdims=True)
            w = jnp.where(front, even, odd)
            t = [jnp.sum(g_ref[h, c] * w, axis=0, keepdims=True) for c in range(6)]
            wide = jnp.concatenate(t[0:4], axis=1)
            half = (iota((1, 4 * BLOCK), 1) & HALF) == 0
            rows = [*thirds(jnp.where(half, wide, 0.0)), *thirds(jnp.where(half, 0.0, wide))]
            rows.append(jnp.zeros((10, 4 * BLOCK), f32))
            found = pick(jnp.concatenate(rows, axis=0).astype(jnp.bfloat16), hot[h])
            turned = [pltpu.roll(x, HALF, axis=1) for x in t[4:6]]
            kept = [jnp.where(front, t[4], turned[1]), jnp.where(front, turned[0], t[5])]
            for s, b in enumerate(ends):
                value = found[3 * s : 3 * s + 1] + found[3 * s + 1 : 3 * s + 2]
                value = value + found[3 * s + 2 : 3 * s + 3]
                for q, cell in enumerate(others(b)):
                    out[cell] = out[cell] + value[:, q * BLOCK : (q + 1) * BLOCK]
                out[OWN[b]] = out[OWN[b]] + kept[s]
        for cell in range(16):
            terms[step, cell : cell + 1, :] = out[cell]

    def fill_kernel():
        parts = [f_ref[:, cell * BLOCK : (cell + 1) * BLOCK] for cell in range(16)]
        turned = [parts[c].T for c in OWN]
        for b in range(4):
            t = turned[b]
            for q, cell in enumerate(around(b)):
                o = parts[cell]
                kern = kernel_value(t[:, 0:1], t[:, 1:2], t[:, 2:3], o[0:1], o[1:2], o[2:3])
                k_ref[b, q] = kern

    def exchange_terms(step):
        args = (terms.at[step], terms_in.at[step], send_t.at[step], recv_t.at[step], terms_cut)
        links.start(*args)
        if step == 0:
            fill_kernel()
        widen(step + 1)
        links.finish(*args)
        for cell in range(16):
            r, c = cell // 4, cell % 4
            value = terms[step, cell : cell + 1, :]
            for k, (dx, dy) in enumerate(DIRS):
                rr, cc = r - 2 * dx, c - 2 * dy
                if 0 <= rr < 4 and 0 <= cc < 4:
                    at = rr * 4 + cc
                    value = value + terms_in[step, k, at : at + 1, :]
            if step == 1:
                value = value - total[0, cell : cell + 1, :]
            total[step, cell : cell + 1, :] = value

    def operate(step):
        diagonal = iota((BLOCK, BLOCK), 0) == iota((BLOCK, BLOCK), 1)
        for b in range(4):
            acc = jnp.zeros((BLOCK, BLOCK), f32)
            for q, cell in enumerate(around(b)):
                acc = acc + k_ref[b, q] * total[step, cell : cell + 1, :]
            down = jnp.sum(acc, axis=1, keepdims=True)
            value = jnp.sum(jnp.where(diagonal, down, 0.0), axis=0, keepdims=True)
            value = value + noise[b] * total[step, OWN[b] : OWN[b] + 1, :]
            image[step, b : b + 1, :] = value

    def line_copy(src, buf, send, recv, peer, at, off):
        return pltpu.make_async_remote_copy(
            src_ref=src,
            dst_ref=buf.at[at],
            send_sem=send.at[off],
            recv_sem=recv.at[off],
            device_id=peer,
            device_id_type=MESH,
        )

    def reduce_line(src, buf, send, recv, peers, me, size):
        copies = [line_copy(src, buf, send, recv, p, me, o) for o, p in enumerate(peers)]
        for copy in copies:
            copy.start()
        buf[me] = src[...]
        for copy in copies:
            copy.wait()
        value = buf[0]
        for at in range(1, size):
            value = value + buf[at]
        return value

    def reduce_all(rows):
        lanes = iota((1, BLOCK), 1)
        packed = jnp.zeros((1, BLOCK), jnp.float32)
        for at, row in enumerate(rows):
            packed = packed + jnp.where(lanes == at, jnp.sum(row, axis=1, keepdims=True), 0.0)
        sums[0] = packed
        value = reduce_line(sums.at[0], sums_y, send_y, recv_y, line_y, me, size)
        if not direct:
            sums[1] = value
            value = reduce_line(sums.at[1], sums_x, send_x, recv_x, line_x, gx, nx)
        return [
            jnp.sum(jnp.where(lanes == at, value, 0.0), axis=1, keepdims=True)
            for at in range(len(rows))
        ]

    def across(left, right):
        value = left[0] * right[0]
        for a, b in zip(left[1:], right[1:]):
            value = value + a * b
        return value

    def mine(ref, step):
        return [ref[step, c : c + 1, :] for c in OWN]

    precondition(0)
    exchange_terms(0)
    operate(0)
    args = (image.at[0], image_in, send_i, recv_i, image_cut)
    links.start(*args)
    first = mine(total, 0)
    along = [image[0, b : b + 1, :] for b in range(4)]
    start = [res[c : c + 1, :] for c in OWN]
    links.finish(*args)
    for cell in range(16):
        way, inner = source_of(cell)
        if way == (0, 0):
            value = image[0, inner : inner + 1, :]
        else:
            value = image_in[DIRS.index(way), inner : inner + 1, :]
        res[cell : cell + 1, :] = value
    precondition(1)
    exchange_terms(1)
    operate(1)
    second = mine(total, 1)
    along2 = [image[1, b : b + 1, :] for b in range(4)]
    base, extra, cross, curve = reduce_all(
        [
            across(first, along),
            across([s - a for s, a in zip(start, along)], first),
            across(along, second),
            across(second, along2),
        ]
    )
    share = extra / base
    alpha = 1.0 + share
    kappa = alpha * cross / base
    alpha2 = (share + kappa) * base / (alpha * (curve - cross * cross / base))
    for b in range(4):
        solved = alpha * first[b] + alpha2 * (kappa * first[b] - alpha * second[b])
        part = slice(b * BLOCK, (b + 1) * BLOCK)
        mean_ref[:, part] = start[b] - noise[b] * solved
        left = start[b] - alpha * along[b]
        res_ref[:, part] = left - alpha2 * (kappa * along[b] - alpha * along2[b])


def local(nx, ny, coords, neighbours, noise_var, observations):
    tile = observations.shape[2]
    line = nx * ny if max(nx, ny) <= 8 else ny
    f32 = jnp.float32
    vmem = pl.BlockSpec(memory_space=pltpu.VMEM)
    dma = pltpu.SemaphoreType.DMA
    whole = pl.BlockSpec(memory_space=pl.ANY)
    mean, residual = pl.pallas_call(
        functools.partial(solve_kernel, nx, ny),
        out_shape=(jax.ShapeDtypeStruct((1, tile), f32),) * 2,
        in_specs=[whole] * 4,
        out_specs=[vmem] * 2,
        scratch_shapes=[
            pltpu.VMEM((8, tile), f32),
            pltpu.VMEM((8, 8, tile), f32),
            pltpu.VMEM((4, NEIGH), jnp.int32),
            pltpu.VMEM((8, 16 * BLOCK), f32),
            pltpu.VMEM((2, 4 * BLOCK, 8 * BLOCK), jnp.bfloat16),
            pltpu.VMEM((2, 6, 6 * HALF, BLOCK), f32),
            pltpu.VMEM((2, 5, 6 * HALF, BLOCK), f32),
            pltpu.VMEM((2, 6, HALF, BLOCK), f32),
            pltpu.VMEM((2, 4, BLOCK, BLOCK), f32),
            pltpu.VMEM((2, 6, BLOCK, BLOCK), f32),
            pltpu.VMEM((2, 8, BLOCK), f32),
            pltpu.VMEM((4, 9, BLOCK, BLOCK), f32),
            pltpu.VMEM((16, BLOCK), f32),
            pltpu.VMEM((2, 16, BLOCK), f32),
            pltpu.VMEM((2, 8, 16, BLOCK), f32),
            pltpu.VMEM((2, 16, BLOCK), f32),
            pltpu.VMEM((2, 8, BLOCK), f32),
            pltpu.VMEM((8, 8, BLOCK), f32),
            pltpu.VMEM((2, 1, BLOCK), f32),
            pltpu.VMEM((line, 1, BLOCK), f32),
            pltpu.VMEM((nx, 1, BLOCK), f32),
            dma((6,)),
            dma((8,)),
            dma((8,)),
            dma((2, 8)),
            dma((2, 8)),
            dma((8,)),
            dma((8,)),
            dma((line,)),
            dma((line,)),
            dma((nx,)),
            dma((nx,)),
            pltpu.SemaphoreType.REGULAR((3,)),
        ],
        compiler_params=pltpu.CompilerParams(
            collective_id=0, has_side_effects=True, vmem_limit_bytes=60 << 20
        ),
        name="solve",
    )(coords, neighbours, noise_var.reshape(1, tile), observations.reshape(1, tile))
    return (mean.reshape(observations.shape), residual.reshape(observations.shape))


def solution(mesh):
    in_specs = (
        P(None, "gx", "gy", None),
        P("gx", "gy", None, None),
        P("gx", "gy", None),
        P("gx", "gy", None),
    )
    out_specs = (P("gx", "gy", None), P("gx", "gy", None))
    body = functools.partial(local, mesh.shape["gx"], mesh.shape["gy"])
    return jax.shard_map(body, mesh=mesh, in_specs=in_specs, out_specs=out_specs, check_vma=False)
```
